32 devices in a mesh: group: 2 (over x), stream: 16 (over z, y, core).
Axes of the slice: x: 2, y: 2, z: 4, core: 2. Of those that a mesh axis runs over, the one named last changes fastest.
Arguments:
- snapshot: float32 [256, 4, 512, 64], P('stream', 'group'), parts along dimension 1, may hold values from -6 to 6
- mode_weight: float32 [32, 32, 64, 128], P('stream'), may hold values from -4 to 4
- local_weight: float32 [64, 64], replicated, may hold values from -0.75 to 0.75
- offset_bias: float32 [64], replicated, may hold values from -4 to 4
- upstream: float32 [256, 4, 512, 64], P('stream', 'group'), parts along dimension 1, may hold values from -6 to 6
Outputs:
- activated: float32 [256, 4, 512, 64], P('stream', 'group'), parts along dimension 1
- grad_snapshot: float32 [256, 4, 512, 64], P('stream', 'group'), parts along dimension 1
- grad_modes: float32 [32, 64, 64, 128], P('stream', 'group'), parts along dimension 1
The draws below stay inside these ranges and needn't reach their ends.
There are 2 independent parts, one for each index of `group`. The reference program is written for one: setup_inputs(seed, part) draws one part's arguments, and reference() takes and returns one part's arrays. A program takes and returns all parts, laid end to end along the dimension named above; an argument that names none is the same for every part. Nothing has to cross between parts.
All inputs are finite; a program needn't handle non-finite values.
Results may differ from the reference program's by a relative error of at most 0.00008.
Values sent between devices are 32-bit elements; how exact they have to be, the bound alone decides.
No kernel may reach another device: no remote copies, remote signals or barrier semaphores. Data moves between devices by JAX's collectives and lax.ppermute only.
A program may use at most 64 MiB of HBM per device.

```python
import math
import jax
import jax.numpy as jnp
from jax import lax

C = 64
MX = 32
MZ = 32
NZ = 512
PLANES = 2
NX = 256


def block_scale(stream_key, shape, pieces, least, high):
    loudness = 1.0
    for axis_at, shards_of in pieces:
        heights = jax.random.uniform(jax.random.fold_in(jax.random.fold_in(stream_key, 6), axis_at), (shards_of,), jnp.float32, least / len(pieces), high / len(pieces))
        loudness = loudness * jnp.repeat(jnp.exp(heights), shape[axis_at] // shards_of).reshape((-1,) + (1,) * (len(shape) - 1 - axis_at))
    return loudness


def normal_values(key, dims, scale, reach, shards=(), held_as=jnp.bfloat16):
    loudness = block_scale(key, dims, shards, -0.22, 0.18) if shards else 1.0
    result = jax.random.normal(key, dims, jnp.float32) * scale * loudness
    return jnp.minimum(jnp.maximum(result, -reach), reach).astype(held_as)


def setup_inputs(seed: int = 0, part: int = 0) -> dict:
    splits = jax.random.split(jax.random.key(seed), 6)
    own_keys = jax.random.split(jax.random.fold_in(splits[5], part), 6)
    snapshot = normal_values(own_keys[0], (NX, PLANES, NZ, C), 1.0, 6.0, ((0, 16),), jnp.float32)
    mode_weight = normal_values(splits[1], (MX, MZ, C, 2 * C), ((4 * MX * MZ * C) // (NX * NZ)) ** -0.5, 4.0, ((0, 16),), jnp.float32)
    local_weight = normal_values(splits[2], (C, C), C ** -0.5, 0.75, (), jnp.float32)
    offset_bias = normal_values(splits[3], (C,), 1.0, 4.0, (), jnp.float32)
    upstream = normal_values(own_keys[4], (NX, PLANES, NZ, C), 1.0, 6.0, ((0, 16),), jnp.float32)
    return dict(snapshot=snapshot, mode_weight=mode_weight, local_weight=local_weight, offset_bias=offset_bias, upstream=upstream)


def hi_einsum(form, left, right):
    return jnp.einsum(form, left, right, precision=lax.Precision.HIGHEST)

def mode_tables(first_row, row_count, total_modes, length, offset, cells):
    rows = first_row + jnp.arange(row_count, dtype=jnp.int32)
    wave = jnp.where(rows < total_modes // 2, rows, rows + length - total_modes)
    points = offset + jnp.arange(cells, dtype=jnp.int32)
    phase = wave[:, None] * points[None, :] % length
    angles = phase.astype(jnp.float32) * (2.0 * math.pi / length)
    return (jnp.cos(angles), jnp.sin(angles))

def span_tables(length, modes, scale):
    points = jnp.arange(length, dtype=jnp.int32)
    waves = jnp.arange(modes, dtype=jnp.int32)
    phase = points[:, None] * waves[None, :] % length
    angles = phase.astype(jnp.float32) * (2.0 * math.pi / length)
    forward = jnp.stack([jnp.cos(angles), -jnp.sin(angles)], axis=2)
    factor = jnp.where(waves == 0, 1.0, 2.0).astype(jnp.float32) / scale
    backward = jnp.stack([jnp.cos(angles).T, -jnp.sin(angles).T], axis=1) * factor[:, None, None]
    return (forward, backward)

def flip_parts(values):
    half = values.shape[-1] // 2
    return jnp.concatenate([values[..., half:], -values[..., :half]], axis=-1)

def flip_back(values):
    half = values.shape[-1] // 2
    return jnp.concatenate([-values[..., half:], values[..., :half]], axis=-1)

def mix_modes(coeffs, weights):
    half = weights.shape[2]
    first = hi_einsum('jbkc,jkcd->jbkd', coeffs[..., :half], weights)
    second = hi_einsum('jbkc,jkcd->jbkd', coeffs[..., half:], weights)
    real_part = first[..., :half] - second[..., half:]
    imag_part = first[..., half:] + second[..., :half]
    return jnp.concatenate([real_part, imag_part], axis=-1)

def mix_adjoint(coeffs, dmixed, weights):
    half = weights.shape[2]
    c_re, c_im = (coeffs[..., :half], coeffs[..., half:])
    d_re, d_im = (dmixed[..., :half], dmixed[..., half:])
    w_re, w_im = (weights[..., :half], weights[..., half:])
    grad_re = hi_einsum('jbkc,jbkd->jkcd', c_re, d_re) + hi_einsum('jbkc,jbkd->jkcd', c_im, d_im)
    grad_im = hi_einsum('jbkc,jbkd->jkcd', c_re, d_im) - hi_einsum('jbkc,jbkd->jkcd', c_im, d_re)
    dmod_re = hi_einsum('jbkd,jkcd->jbkc', d_re, w_re) + hi_einsum('jbkd,jkcd->jbkc', d_im, w_im)
    dmod_im = hi_einsum('jbkd,jkcd->jbkc', d_im, w_re) - hi_einsum('jbkd,jkcd->jbkc', d_re, w_im)
    return (jnp.concatenate([grad_re, grad_im], axis=-1), jnp.concatenate([dmod_re, dmod_im], axis=-1))

def gelu_slope(values):
    return 0.5 * (1.0 + jax.scipy.special.erf(values / math.sqrt(2.0))) + values * jnp.exp(-0.5 * values * values) / math.sqrt(2.0 * math.pi)

def reference(snapshot, mode_weight, local_weight, offset_bias, upstream):
    cos_rows, sin_rows = mode_tables(0, MX, MX, NX, 0, NX)
    span_fwd, span_inv = span_tables(NZ, MZ, float(NX * NZ))
    spanwise = hi_einsum('xbzc,zkp->xbkpc', snapshot, span_fwd).reshape(NX, PLANES, MZ, 2 * C)
    modes = hi_einsum('jx,xbkq->jbkq', cos_rows, spanwise) + hi_einsum('jx,xbkq->jbkq', sin_rows, flip_parts(spanwise))
    mixed = mix_modes(modes, mode_weight)
    inverse = hi_einsum('jx,jbkq->xbkq', cos_rows, mixed) + hi_einsum('jx,jbkq->xbkq', sin_rows, flip_back(mixed))
    spectral = hi_einsum('xbkpo,kpz->xbzo', inverse.reshape(NX, PLANES, MZ, 2, C), span_inv)
    pre = spectral + hi_einsum('xbzc,cd->xbzd', snapshot, local_weight) + offset_bias
    activated = jax.nn.gelu(pre, approximate=False)
    dpre = upstream * gelu_slope(pre)
    dinverse = hi_einsum('xbzo,kpz->xbkpo', dpre, span_inv).reshape(NX, PLANES, MZ, 2 * C)
    dmixed = hi_einsum('jx,xbkq->jbkq', cos_rows, dinverse) + flip_parts(hi_einsum('jx,xbkq->jbkq', sin_rows, dinverse))
    grad_modes, dmodes = mix_adjoint(modes, dmixed, mode_weight)
    dspanwise = hi_einsum('jx,jbkq->xbkq', cos_rows, dmodes) + flip_back(hi_einsum('jx,jbkq->xbkq', sin_rows, dmodes))
    grad_snapshot = hi_einsum('xbkpc,zkp->xbzc', dspanwise.reshape(NX, PLANES, MZ, 2, C), span_fwd)
    grad_snapshot = grad_snapshot + hi_einsum('xbzo,co->xbzc', dpre, local_weight)
    return (activated, grad_snapshot, grad_modes)
```

```python
import math

import jax
import jax.numpy as jnp
from jax import lax
from jax.sharding import PartitionSpec as P


def hi_einsum(form, left, right):
    return jnp.einsum(form, left, right, precision=lax.Precision.HIGHEST)


def swap(values, bit):
    count = lax.axis_size("stream")
    return lax.ppermute(values, "stream", [(i, i ^ bit) for i in range(count)])


def stage_bits():
    count = lax.axis_size("stream")
    bits = [1 << i for i in range(count.bit_length() - 1)]
    assert 1 << len(bits) == count
    return bits


def held_rows(owned):
    bits = stage_bits()
    pattern = [0]
    for bit in reversed(bits):
        pattern = pattern + [p | bit for p in pattern]
    blocks = jnp.asarray(pattern, jnp.int32) ^ lax.axis_index("stream")
    return (blocks[:, None] * owned + jnp.arange(owned, dtype=jnp.int32)[None, :]).reshape(-1)


def scatter_sum(values):
    for bit in stage_bits():
        half = values.shape[0] // 2
        values = values[:half] + swap(values[half:], bit)
    return values


def gather_all(values):
    for bit in reversed(stage_bits()):
        values = jnp.concatenate([values, swap(values, bit)], axis=0)
    return values


def mode_tables(rows, total_modes, length, offset, cells):
    wave = jnp.where(rows < total_modes // 2, rows, rows + length - total_modes)
    points = offset + jnp.arange(cells, dtype=jnp.int32)
    phase = wave[:, None] * points[None, :] % length
    angles = phase.astype(jnp.float32) * (2.0 * math.pi / length)
    return (jnp.cos(angles), jnp.sin(angles))


def span_tables(length, modes, scale):
    points = jnp.arange(length, dtype=jnp.int32)
    waves = jnp.arange(modes, dtype=jnp.int32)
    phase = points[:, None] * waves[None, :] % length
    angles = phase.astype(jnp.float32) * (2.0 * math.pi / length)
    forward = jnp.stack([jnp.cos(angles), -jnp.sin(angles)], axis=2)
    factor = jnp.where(waves == 0, 1.0, 2.0).astype(jnp.float32) / scale
    backward = jnp.stack([jnp.cos(angles).T, -jnp.sin(angles).T], axis=1) * factor[:, None, None]
    return (forward, backward)


def flip_parts(values):
    half = values.shape[-1] // 2
    return jnp.concatenate([values[..., half:], -values[..., :half]], axis=-1)


def flip_back(values):
    half = values.shape[-1] // 2
    return jnp.concatenate([-values[..., half:], values[..., :half]], axis=-1)


def mix_modes(coeffs, weights):
    half = weights.shape[2]
    first = hi_einsum("jbkc,jkcd->jbkd", coeffs[..., :half], weights)
    second = hi_einsum("jbkc,jkcd->jbkd", coeffs[..., half:], weights)
    real_part = first[..., :half] - second[..., half:]
    imag_part = first[..., half:] + second[..., :half]
    return jnp.concatenate([real_part, imag_part], axis=-1)


def mix_adjoint(coeffs, dmixed, weights):
    half = weights.shape[2]
    c_re, c_im = (coeffs[..., :half], coeffs[..., half:])
    d_re, d_im = (dmixed[..., :half], dmixed[..., half:])
    w_re, w_im = (weights[..., :half], weights[..., half:])
    grad_re = hi_einsum("jbkc,jbkd->jkcd", c_re, d_re) + hi_einsum("jbkc,jbkd->jkcd", c_im, d_im)
    grad_im = hi_einsum("jbkc,jbkd->jkcd", c_re, d_im) - hi_einsum("jbkc,jbkd->jkcd", c_im, d_re)
    dmod_re = hi_einsum("jbkd,jkcd->jbkc", d_re, w_re) + hi_einsum("jbkd,jkcd->jbkc", d_im, w_im)
    dmod_im = hi_einsum("jbkd,jkcd->jbkc", d_im, w_re) - hi_einsum("jbkd,jkcd->jbkc", d_re, w_im)
    return (
        jnp.concatenate([grad_re, grad_im], axis=-1),
        jnp.concatenate([dmod_re, dmod_im], axis=-1),
    )


def gelu_slope(values):
    return 0.5 * (1.0 + jax.scipy.special.erf(values / math.sqrt(2.0))) + values * jnp.exp(
        -0.5 * values * values
    ) / math.sqrt(2.0 * math.pi)


def per_device(snapshot, mode_weight, local_weight, offset_bias, upstream):
    cells, planes, span_len, channels = snapshot.shape
    devices = lax.axis_size("stream")
    owned = mode_weight.shape[0]
    span_modes = mode_weight.shape[1]
    total_modes = owned * devices
    stream_len = cells * devices
    offset = lax.axis_index("stream") * cells
    span_fwd, span_inv = span_tables(span_len, span_modes, float(stream_len * span_len))
    spanwise = hi_einsum("xbzc,zkp->xbkpc", snapshot, span_fwd).reshape(
        cells, planes, span_modes, 2 * channels
    )
    spanwise_flip = flip_parts(spanwise)
    rows = held_rows(owned)
    cos_rows, sin_rows = mode_tables(rows, total_modes, stream_len, offset, cells)
    modes = scatter_sum(
        hi_einsum("jx,xbkq->jbkq", cos_rows, spanwise)
        + hi_einsum("jx,xbkq->jbkq", sin_rows, spanwise_flip)
    )
    mixed = mix_modes(modes, mode_weight)
    shards = gather_all(mixed)
    inverse = hi_einsum("jx,jbkq->xbkq", cos_rows, shards) + hi_einsum(
        "jx,jbkq->xbkq", sin_rows, flip_back(shards)
    )
    spectral = hi_einsum(
        "xbkpo,kpz->xbzo", inverse.reshape(cells, planes, span_modes, 2, channels), span_inv
    )
    pre = spectral + hi_einsum("xbzc,cd->xbzd", snapshot, local_weight) + offset_bias
    activated = jax.nn.gelu(pre, approximate=False)
    dpre = upstream * gelu_slope(pre)
    dinverse = hi_einsum("xbzo,kpz->xbkpo", dpre, span_inv).reshape(
        cells, planes, span_modes, 2 * channels
    )
    dmixed = scatter_sum(
        hi_einsum("jx,xbkq->jbkq", cos_rows, dinverse)
        + flip_parts(hi_einsum("jx,xbkq->jbkq", sin_rows, dinverse))
    )
    grad_modes, dmodes = mix_adjoint(modes, dmixed, mode_weight)
    shards = gather_all(dmodes)
    dspanwise = hi_einsum("jx,jbkq->xbkq", cos_rows, shards) + flip_back(
        hi_einsum("jx,jbkq->xbkq", sin_rows, shards)
    )
    grad_snapshot = hi_einsum(
        "xbkpc,zkp->xbzc", dspanwise.reshape(cells, planes, span_modes, 2, channels), span_fwd
    )
    grad_snapshot = grad_snapshot + hi_einsum("xbzo,co->xbzc", dpre, local_weight)
    return (activated, grad_snapshot, grad_modes)


def solution(mesh):
    placed = (
        P("stream", "group", None, None),
        P("stream", None, None, None),
        P(),
        P(),
        P("stream", "group", None, None),
    )
    return jax.shard_map(
        per_device,
        mesh=mesh,
        in_specs=placed,
        out_specs=(
            P("stream", "group", None, None),
            P("stream", "group", None, None),
            P("stream", "group", None, None),
        ),
        check_vma=False,
    )
```

```python
import functools
import math

import jax
import jax.numpy as jnp
import numpy as np
from jax import lax
from jax.experimental import pallas as pl
from jax.experimental.pallas import tpu as pltpu
from jax.sharding import PartitionSpec as P

F32 = jnp.float32
BF16 = jnp.bfloat16
LANES = 128
SUB = 8
VMEM_LIMIT = 48 << 20


def split_np(values):
    values = values.astype(np.float32)
    high = values.astype(BF16)
    low = (values - high.astype(np.float32)).astype(BF16)
    return high, low


def span_tables(length, modes, scale):
    angle = 2.0 * np.pi * (np.outer(np.arange(length), np.arange(modes)) % length) / length
    forward = np.concatenate([np.cos(angle), -np.sin(angle)], axis=1)
    factor = np.where(np.arange(modes) == 0, 1.0, 2.0) / scale
    backward = forward * np.concatenate([factor, factor])[None, :]

    def analysis(table):
        flipped = np.concatenate([table[:, modes:], -table[:, :modes]], axis=1)
        both = np.concatenate([table, flipped], axis=1)
        return np.concatenate(split_np(both), axis=1)

    def synthesis(table):
        return np.concatenate(split_np(table.T), axis=0)

    return analysis(forward), analysis(backward), synthesis(forward), synthesis(backward)


def stage_bits():
    count = lax.axis_size("stream")
    bits = [1 << i for i in range(count.bit_length() - 1)]
    assert 1 << len(bits) == count
    return bits


def stream_tables(owned, total_modes, cells):
    me = lax.axis_index("stream")
    pattern = [0]
    for bit in reversed(stage_bits()):
        pattern = pattern + [p | bit for p in pattern]
    length = cells * lax.axis_size("stream")
    pattern = np.repeat(np.asarray(pattern, np.int32), owned)
    inner = np.tile(np.arange(owned, dtype=np.int32), total_modes // owned)

    def angles(pattern, inner, cell):
        rows = (pattern ^ me) * owned + inner
        wave = jnp.where(rows < total_modes // 2, rows, rows + length - total_modes)
        phase = wave * (me * cells + cell) % length
        return phase.astype(F32) * (2.0 * math.pi / length)

    lane = np.arange(2 * cells * SUB)
    down = angles(pattern[:, None], inner[:, None], (lane[None, :] // SUB % cells).astype(np.int32))
    down = jnp.where(lane[None, :] < cells * SUB, jnp.cos(down), jnp.sin(down))
    row = np.arange(2 * cells)
    up = angles(
        np.repeat(pattern, SUB)[None, :],
        np.repeat(inner, SUB)[None, :],
        (row[:, None] % cells).astype(np.int32),
    )
    up = jnp.where(row[:, None] < cells, jnp.cos(up), jnp.sin(up))
    return down, up


def split(values):
    high = values.astype(BF16)
    return high, (values - high.astype(F32)).astype(BF16)


def dot(left, right):
    return jnp.dot(left, right, preferred_element_type=F32)


def expand_table(table_ref, scratch_ref):
    rows, lanes = table_ref.shape
    full = jnp.broadcast_to(table_ref[...][:, None, :], (rows, SUB, lanes)).reshape(rows * SUB, lanes)
    row = lax.broadcasted_iota(jnp.int32, full.shape, 0) % SUB
    lane = lax.broadcasted_iota(jnp.int32, full.shape, 1) % SUB
    high, low = split(jnp.where(row == lane, full, 0.0))
    scratch_ref[0] = high
    scratch_ref[1] = low


def analyse(values_high, values_low, table_ref, at, coef_ref):
    full = dot(values_high, table_ref[...])
    full = full[:, :LANES] + full[:, LANES:] + dot(values_low, table_ref[:, :LANES])
    cells = coef_ref.shape[1] // (2 * SUB)
    half = 4 * SUB
    low_lane = lax.broadcasted_iota(jnp.int32, (half, LANES), 1) < LANES // 2
    for i in range(full.shape[0] // (2 * half)):
        low = full[2 * half * i : 2 * half * i + half]
        high = full[2 * half * i + half : 2 * half * (i + 1)]
        plain = jnp.where(low_lane, low, pltpu.roll(high, LANES // 2, 1))
        flipped = jnp.where(low_lane, pltpu.roll(low, LANES // 2, 1), high)
        for block in range(half // SUB):
            rows = slice(SUB * block, SUB * (block + 1))
            coef_ref[block, pl.ds(pl.multiple_of((at + i) * SUB, SUB), SUB)] = plain[rows]
            coef_ref[block, pl.ds(pl.multiple_of((cells + at + i) * SUB, SUB), SUB)] = flipped[rows]


def to_modes(coef_ref, table_ref, keep_ref, send_ref):
    modes = 2 * keep_ref.shape[0]
    for block in range(coef_ref.shape[0]):
        high, low = split(coef_ref[block])
        full = dot(table_ref[0], jnp.concatenate([high, low], axis=1))
        full = full[:, :LANES] + full[:, LANES:] + dot(table_ref[1], high)
        full = full.reshape(modes, SUB, LANES)
        rows = slice(SUB * block, SUB * (block + 1))
        keep_ref[:, 0, rows] = full[: modes // 2]
        send_ref[:, 0, rows] = full[modes // 2 :]


def from_modes(front_ref, back_ref, table_ref, inv_ref):
    modes = 2 * front_ref.shape[0]
    cells = inv_ref.shape[0]
    lane = lax.broadcasted_iota(jnp.int32, (cells * SUB, LANES), 1)
    real = lane % (LANES // 2) < LANES // 4
    for block in range(inv_ref.shape[1] // SUB):
        rows = slice(SUB * block, SUB * (block + 1))
        values = jnp.concatenate([front_ref[:, 0, rows], back_ref[:, 0, rows]], axis=0)
        high, low = split(values.reshape(modes * SUB, LANES))
        full = dot(table_ref[0], jnp.concatenate([high, low], axis=1))
        full = full[:, :LANES] + full[:, LANES:] + dot(table_ref[1], high)
        plain, other = full[: cells * SUB], full[cells * SUB :]
        turned = jnp.where(
            real, -pltpu.roll(other, 3 * LANES // 4, 1), pltpu.roll(other, LANES // 4, 1)
        )
        inv_ref[:, rows] = (plain + turned).reshape(cells, SUB, LANES)


def synthesise(inv, weight, table_ref, high, low):
    half = inv.shape[0]
    low_lane = lax.broadcasted_iota(jnp.int32, (half, LANES), 1) < LANES // 2
    first = jnp.where(low_lane, inv, weight[:half])
    second = jnp.where(low_lane, pltpu.roll(inv, LANES // 2, 1), weight[half:])
    lhs_high, lhs_low = split(jnp.concatenate([first, second], axis=0))
    lhs = jnp.concatenate(
        [
            jnp.concatenate([lhs_high, lhs_high], axis=1),
            jnp.concatenate([lhs_low, jnp.zeros_like(lhs_low)], axis=1),
        ],
        axis=0,
    )
    width = LANES // 2
    rhs = jnp.concatenate([table_ref[:width], high, table_ref[width:], low], axis=0)
    full = dot(lhs, rhs)
    return full[: 2 * half] + full[2 * half :]


def normal_parts(values):
    density = jnp.exp(-0.5 * values * values) * (1.0 / math.sqrt(2.0 * math.pi))
    return 0.5 * (1.0 + lax.erf(values * (1.0 / math.sqrt(2.0)))), density


def transpose_out(rows):
    parts = []
    for half in range(2):
        for part in range(2):
            shift = part * (LANES // 2) + half * (LANES // 4)
            parts.append(pltpu.roll(rows, LANES - shift, 1) if shift else rows)
    return jnp.concatenate(parts, axis=0).T[: LANES // 4]


def transpose_in(values):
    quarter = LANES // 4
    turned = jnp.concatenate([values] * 4, axis=0).T
    lane = lax.broadcasted_iota(jnp.int32, (quarter, LANES), 1) // quarter
    result = turned[:quarter]
    for half in range(2):
        for part in range(2):
            rows = turned[quarter * (2 * half + part) : quarter * (2 * half + part + 1)]
            result = jnp.where(lane == 2 * part + half, rows, result)
    return result


def turn_down(rows):
    lane = lax.broadcasted_iota(jnp.int32, rows.shape, 1) < LANES // 2
    rolled = pltpu.roll(rows, LANES // 2, 1)
    return jnp.where(lane, rolled, -rolled)


def spanwise_kernel(x_ref, table_ref, down_ref, keep_ref, send_ref, coef_ref, down_scr):
    step = pl.program_id(1)
    cells, _, channels, span = x_ref.shape

    @pl.when((step == 0) & (pl.program_id(0) == 0))
    def _():
        expand_table(down_ref, down_scr)

    high, low = split(x_ref[...].reshape(cells * channels, span))
    analyse(high, low, table_ref, step * cells, coef_ref)

    @pl.when(step == pl.num_programs(1) - 1)
    def _():
        to_modes(coef_ref, down_scr, keep_ref, send_ref)


def mix_kernel(*refs):
    *piece_refs, w_ref, modes_ref, mixed_ref, first_scr, second_scr = refs
    planes = modes_ref.shape[1]
    kz_count = w_ref.shape[1]
    quarter = LANES // 4
    for plane in range(planes):
        total = piece_refs[0][0, plane]
        for ref in piece_refs[1:]:
            total = total + ref[0, plane]
        modes_ref[0, plane] = total
        for kz in range(kz_count):
            sums = [None, None]
            for half in range(2):
                weight = w_ref[0, kz, quarter * half : quarter * (half + 1)]
                for part in range(2):
                    at = half * (LANES // 2) + part * quarter + kz
                    term = total[:, at : at + 1] * weight
                    sums[part] = term if sums[part] is None else sums[part] + term
            first_scr[kz : kz + 1] = jnp.sum(sums[0], axis=0, keepdims=True)
            second_scr[kz : kz + 1] = jnp.sum(sums[1], axis=0, keepdims=True)
        rows = first_scr[...] - turn_down(second_scr[...])
        mixed_ref[0, plane] = transpose_out(rows)


def middle_kernel(
    x_ref, up_ref, front_ref, back_ref, local_ref, bias_ref, synth_ref, table_ref,
    down_ref, back_table_ref, *rest
):
    act_ref, dpre_ref, keep_ref, send_ref, inv_ref, coef_ref, down_scr, back_scr = rest[-8:]
    step = pl.program_id(1)
    cells, _, channels, span = x_ref.shape

    @pl.when((step == 0) & (pl.program_id(0) == 0))
    def _():
        expand_table(down_ref, down_scr)
        expand_table(back_table_ref, back_scr)

    @pl.when(step == 0)
    def _():
        from_modes(front_ref, back_ref, back_scr, inv_ref)

    for cell in range(cells):
        high, low = split(x_ref[cell, 0])
        pre = synthesise(inv_ref[step * cells + cell], local_ref[...], synth_ref, high, low)
        pre = pre + bias_ref[...]
        cumulative, density = normal_parts(pre)
        act_ref[cell, 0] = pre * cumulative
        dpre = up_ref[cell, 0] * (cumulative + pre * density)
        dpre_ref[cell, 0] = dpre
        high, low = split(dpre)
        analyse(high, low, table_ref, step * cells + cell, coef_ref)

    @pl.when(step == pl.num_programs(1) - 1)
    def _():
        to_modes(coef_ref, down_scr, keep_ref, send_ref)


def adjoint_kernel(*refs):
    *piece_refs, w_ref, dmixed_ref, dmodes_ref = refs
    planes = dmixed_ref.shape[1]
    kz_count, channels, width = w_ref.shape[1:]
    quarter = LANES // 4
    weight = w_ref[0].reshape(kz_count * channels, width)
    w_high, w_low = split(weight)
    lane = lax.broadcasted_iota(jnp.int32, (channels, LANES // 2), 1) % quarter
    for plane in range(planes):
        total = piece_refs[0][0, plane]
        for ref in piece_refs[1:]:
            total = total + ref[0, plane]
        dmixed_ref[0, plane] = total
        rows = transpose_in(total)
        both = jnp.concatenate([rows, turn_down(rows)], axis=0)
        high, low = split(both)
        right = jnp.concatenate([high, low], axis=0).T
        full = dot(w_high, right)
        full = full[:, : LANES // 2] + full[:, LANES // 2 :] + dot(w_low, right[:, : LANES // 2])
        full = full.reshape(kz_count, channels, LANES // 2)
        result = jnp.zeros((channels, LANES // 2), F32)
        for kz in range(kz_count):
            result = jnp.where(lane == kz, full[kz], result)
        dmodes_ref[0, plane] = jnp.concatenate(
            [result[: channels // 2], result[channels // 2 :]], axis=1
        )


def weight_grad_kernel(modes_ref, dmixed_ref, grad_ref, rows_scr):
    planes = modes_ref.shape[1]
    kz_count = grad_ref.shape[1]
    quarter = LANES // 4
    for plane in range(planes):
        rows = transpose_in(dmixed_ref[0, plane])
        rows_scr[2 * plane] = rows
        rows_scr[2 * plane + 1] = turn_down(rows)
    for kz in range(kz_count):
        for half in range(2):
            total = None
            for plane in range(planes):
                for part in range(2):
                    at = half * (LANES // 2) + part * quarter + kz
                    column = modes_ref[0, plane, :, at : at + 1]
                    term = column * rows_scr[2 * plane + part, kz : kz + 1]
                    total = term if total is None else total + term
            grad_ref[0, kz, quarter * half : quarter * (half + 1)] = total


def input_grad_kernel(dpre_ref, front_ref, back_ref, local_ref, synth_ref, back_table_ref, *rest):
    out_ref, inv_ref, back_scr = rest[-3:]
    step = pl.program_id(1)
    cells = dpre_ref.shape[0]

    @pl.when((step == 0) & (pl.program_id(0) == 0))
    def _():
        expand_table(back_table_ref, back_scr)

    @pl.when(step == 0)
    def _():
        from_modes(front_ref, back_ref, back_scr, inv_ref)

    for cell in range(cells):
        high, low = split(dpre_ref[cell, 0])
        out_ref[cell, 0] = synthesise(
            inv_ref[step * cells + cell], local_ref[...], synth_ref, high, low
        )


def swap(values, bit):
    count = lax.axis_size("stream")
    return lax.ppermute(values, "stream", [(i, i ^ bit) for i in range(count)])


def scatter_sum(keep, send):
    bits = stage_bits()
    pieces = [keep, swap(send, bits[0])]
    half = keep.shape[0]
    for bit in bits[1:]:
        half //= 2
        part = pieces[0][half : 2 * half]
        for piece in pieces[1:]:
            part = part + piece[half : 2 * half]
        pieces.append(swap(part, bit))
    return pieces


def gather_all(values):
    bits = stage_bits()
    for bit in reversed(bits[1:]):
        values = jnp.concatenate([values, swap(values, bit)], axis=0)
    return values, swap(values, bits[0])


def params():
    return pltpu.CompilerParams(vmem_limit_bytes=VMEM_LIMIT)


def whole(array):
    rank = len(array.shape)
    return pl.BlockSpec(array.shape, lambda *_: (0,) * rank)


def per_device(snapshot, mode_weight, local_weight, offset_bias, upstream):
    cells, planes, span, channels = snapshot.shape
    owned, kz_count = mode_weight.shape[:2]
    total_modes = owned * lax.axis_size("stream")
    half_modes = total_modes // 2
    half_channels = channels // 2
    shape = jax.ShapeDtypeStruct
    x = jnp.swapaxes(snapshot, 2, 3)
    up = jnp.swapaxes(upstream, 2, 3)
    scale = float(cells * lax.axis_size("stream") * span)
    ana_fwd, ana_inv, syn_fwd, syn_inv = map(jnp.asarray, span_tables(span, kz_count, scale))
    down, back = stream_tables(owned, total_modes, cells)
    zeros = jnp.zeros((channels, LANES // 2), F32)
    local_out = jnp.concatenate([zeros, local_weight.T], axis=1)
    local_in = jnp.concatenate([zeros, local_weight], axis=1)
    bias = jnp.broadcast_to(offset_bias[:, None], (channels, span))
    step_cells = 4
    steps = cells // step_cells
    groups = [tuple(range(planes))]
    coef_scr = pltpu.VMEM((half_channels // SUB, 2 * cells * SUB, LANES), F32)
    inv_scr = pltpu.VMEM((cells, half_channels, LANES), F32)
    down_scr = pltpu.VMEM((2, total_modes * SUB, 2 * cells * SUB), BF16)
    back_scr = pltpu.VMEM((2, 2 * cells * SUB, total_modes * SUB), BF16)

    def grid_block(first):
        return pl.BlockSpec((step_cells, 1, channels, span), lambda p, s: (s, first + p, 0, 0))

    half_block = pl.BlockSpec((half_modes, 1, half_channels, LANES), lambda p, s: (0, p, 0, 0))
    any_block = pl.BlockSpec(memory_space=pl.ANY)

    def own_block(count):
        return pl.BlockSpec((1, count, half_channels, LANES), lambda j: (j, 0, 0, 0))

    def own_shape(count):
        return shape((owned, count, half_channels, LANES), F32)

    def half_shape(count):
        return shape((half_modes, count, half_channels, LANES), F32)

    weight_block = pl.BlockSpec((1, kz_count, channels, 2 * channels), lambda j: (j, 0, 0, 0))
    act = grad_snapshot = None
    modes_all, dmixed_all, late = [], [], []
    for group in groups:
        count, first = len(group), group[0]
        keep, send = pl.pallas_call(
            spanwise_kernel,
            grid=(count, steps),
            in_specs=[grid_block(first), whole(ana_fwd), whole(down)],
            out_specs=[half_block, half_block],
            out_shape=[half_shape(count)] * 2,
            scratch_shapes=[coef_scr, down_scr],
            compiler_params=params(),
            name="spanwise",
        )(x, ana_fwd, down)
        pieces = scatter_sum(keep, send)
        modes, mixed = pl.pallas_call(
            mix_kernel,
            grid=(owned,),
            in_specs=[own_block(count)] * len(pieces) + [weight_block],
            out_specs=[own_block(count)] * 2,
            out_shape=[own_shape(count)] * 2,
            scratch_shapes=[pltpu.VMEM((kz_count, LANES), F32)] * 2,
            compiler_params=params(),
            name="mix",
        )(*pieces, mode_weight)
        modes_all.append(modes)
        front, behind = gather_all(mixed)
        extra = [] if act is None else [act]
        act, dpre, keep, send = pl.pallas_call(
            middle_kernel,
            grid=(count, steps),
            in_specs=[
                grid_block(first), grid_block(first), half_block, half_block, whole(local_out),
                whole(bias), whole(syn_inv), whole(ana_inv), whole(down), whole(back),
            ] + [any_block] * len(extra),
            out_specs=[grid_block(first), grid_block(0), half_block, half_block],
            out_shape=[shape(x.shape, F32), shape((cells, count, channels, span), F32)]
            + [half_shape(count)] * 2,
            scratch_shapes=[inv_scr, coef_scr, down_scr, back_scr],
            input_output_aliases={10: 0} if extra else {},
            compiler_params=params(),
            name="middle",
        )(x, up, front, behind, local_out, bias, syn_inv, ana_inv, down, back, *extra)
        pieces = scatter_sum(keep, send)
        dmixed, dmodes = pl.pallas_call(
            adjoint_kernel,
            grid=(owned,),
            in_specs=[own_block(count)] * len(pieces) + [weight_block],
            out_specs=[own_block(count)] * 2,
            out_shape=[own_shape(count)] * 2,
            compiler_params=params(),
            name="adjoint",
        )(*pieces, mode_weight)
        dmixed_all.append(dmixed)
        front, behind = gather_all(dmodes)
        extra = [] if grad_snapshot is None else [grad_snapshot]
        grad_snapshot = pl.pallas_call(
            input_grad_kernel,
            grid=(count, steps),
            in_specs=[
                grid_block(0), half_block, half_block, whole(local_in), whole(syn_fwd), whole(back),
            ] + [any_block] * len(extra),
            out_specs=grid_block(first),
            out_shape=shape(x.shape, F32),
            scratch_shapes=[inv_scr, back_scr],
            input_output_aliases={6: 0} if extra else {},
            compiler_params=params(),
            name="input_grad",
        )(dpre, front, behind, local_in, syn_fwd, back, *extra)
    modes = modes_all[0] if len(groups) == 1 else jnp.concatenate(modes_all, axis=1)
    dmixed = dmixed_all[0] if len(groups) == 1 else jnp.concatenate(dmixed_all, axis=1)
    grad_modes = pl.pallas_call(
        weight_grad_kernel,
        grid=(owned,),
        in_specs=[own_block(planes)] * 2,
        out_specs=weight_block,
        out_shape=shape(mode_weight.shape, F32),
        scratch_shapes=[pltpu.VMEM((2 * planes, kz_count, LANES), F32)],
        compiler_params=params(),
        name="weight_grad",
    )(modes, dmixed)
    return jnp.swapaxes(act, 2, 3), jnp.swapaxes(grad_snapshot, 2, 3), grad_modes


def solution(mesh):
    wide = P("stream", "group", None, None)
    return jax.shard_map(
        per_device,
        mesh=mesh,
        in_specs=(wide, P("stream", None, None, None), P(), P(), wide),
        out_specs=(wide, wide, wide),
        check_vma=False,
    )
```

```python
import functools
import math

import jax
import jax.numpy as jnp
import numpy as np
from jax import lax
from jax.experimental import pallas as pl
from jax.experimental.pallas import tpu as pltpu
from jax.sharding import PartitionSpec as P

F32 = jnp.float32
BF16 = jnp.bfloat16
LANES = 128
SUB = 8
VMEM_LIMIT = 16 << 20


def split_np(values):
    values = values.astype(np.float32)
    high = values.astype(BF16)
    low = (values - high.astype(np.float32)).astype(BF16)
    return high, low


def span_tables(length, modes, scale):
    angle = 2.0 * np.pi * (np.outer(np.arange(length), np.arange(modes)) % length) / length
    forward = np.concatenate([np.cos(angle), -np.sin(angle)], axis=1)
    factor = np.where(np.arange(modes) == 0, 1.0, 2.0) / scale
    backward = forward * np.concatenate([factor, factor])[None, :]

    def analysis(table):
        flipped = np.concatenate([table[:, modes:], -table[:, :modes]], axis=1)
        both = np.concatenate([table, flipped], axis=1)
        return np.concatenate(split_np(both), axis=1)

    def synthesis(table):
        high, low = split_np(table.T)
        return np.concatenate([high, low, high, np.zeros_like(high)], axis=0)

    return analysis(forward), analysis(backward), synthesis(forward), synthesis(backward)


def stage_masks():
    count = lax.axis_size("stream")
    bits = count.bit_length() - 1
    assert 1 << bits == count
    return [1] + [1 << i | 1 for i in range(1, bits)]


def stage_class(index):
    return (index ^ index >> 1 ^ index >> 2) & 1


def stage_mask(index, step):
    masks = stage_masks()
    if len(masks) > 2 and step in (1, 2) and stage_class(index):
        step = 3 - step
    return masks[step]


def mode_angles(position, inner, cell, owned, total_modes, cells):
    me = lax.axis_index("stream")
    masks = stage_masks()
    steps = len(masks)
    length = cells * (1 << steps)
    assert length & (length - 1) == 0
    bits = [position >> (steps - 1 - step) & 1 for step in range(steps)]
    if steps > 2:
        other = (bits[0] ^ stage_class(me)) & 1
        bits[1], bits[2] = (
            jnp.where(other == 1, bits[2], bits[1]),
            jnp.where(other == 1, bits[1], bits[2]),
        )
    block = jnp.zeros_like(position) + me
    for bit, mask in zip(bits, masks):
        block = block ^ bit * mask
    rows = block * owned + inner
    wave = jnp.where(rows < total_modes // 2, rows, rows - total_modes)
    phase = wave * (me * cells + cell) & (length - 1)
    phase = jnp.where(phase > length // 2, phase - length, phase)
    return phase.astype(F32) * (2.0 * math.pi / length)


def split(values):
    high = values.astype(BF16)
    return high, (values - high.astype(F32)).astype(BF16)


def dot(left, right):
    return jnp.dot(left, right, preferred_element_type=F32)


def make_tables(down_ref, back_ref, owned, total_modes, cells):
    def iota(shape, axis):
        return lax.broadcasted_iota(jnp.int32, shape, axis)

    def expand(table, ref):
        rows, lanes = table.shape
        full = jnp.broadcast_to(table[:, None, :], (rows, SUB, lanes)).reshape(rows * SUB, lanes)
        same = (iota(full.shape, 0) & (SUB - 1)) == (iota(full.shape, 1) & (SUB - 1))
        high, low = split(jnp.where(same, full, 0.0))
        ref[0] = high
        ref[1] = low

    def table(shape, mode_axis):
        mode = iota(shape, mode_axis)
        cell = iota(shape, 1 - mode_axis)
        if mode_axis == 1:
            mode = mode >> 3
        else:
            cell = cell >> 3
        shift = owned.bit_length() - 1
        angles = mode_angles(
            mode >> shift, mode & (owned - 1), cell & (cells - 1), owned, total_modes, cells
        )
        return jnp.where(cell < cells, jnp.cos(angles), jnp.sin(angles))

    expand(table((total_modes, 2 * cells * SUB), 0), down_ref)
    expand(table((2 * cells, total_modes * SUB), 1), back_ref)


def analyse(values_high, values_low, table_ref, at, coef_ref):
    full = dot(values_high, table_ref[...])
    full = full[:, :LANES] + full[:, LANES:] + dot(values_low, table_ref[:, :LANES])
    cells = coef_ref.shape[1] // (2 * SUB)
    half = 4 * SUB
    low_lane = lax.broadcasted_iota(jnp.int32, (half, LANES), 1) < LANES // 2
    for i in range(full.shape[0] // (2 * half)):
        low = full[2 * half * i : 2 * half * i + half]
        high = full[2 * half * i + half : 2 * half * (i + 1)]
        plain = jnp.where(low_lane, low, pltpu.roll(high, LANES // 2, 1))
        flipped = jnp.where(low_lane, pltpu.roll(low, LANES // 2, 1), high)
        for block in range(half // SUB):
            rows = slice(SUB * block, SUB * (block + 1))
            coef_ref[block, pl.ds(pl.multiple_of((at + i) * SUB, SUB), SUB)] = plain[rows]
            coef_ref[block, pl.ds(pl.multiple_of((cells + at + i) * SUB, SUB), SUB)] = flipped[rows]


def to_modes(coef_ref, table_ref, keep_ref, send_ref):
    modes = 2 * keep_ref.shape[0]
    for block in range(coef_ref.shape[0]):
        high, low = split(coef_ref[block])
        full = dot(table_ref[0], jnp.concatenate([high, low], axis=1))
        full = full[:, :LANES] + full[:, LANES:] + dot(table_ref[1], high)
        full = full.reshape(modes, SUB, LANES)
        rows = slice(SUB * block, SUB * (block + 1))
        keep_ref[:, 0, rows] = full[: modes // 2]
        send_ref[:, 0, rows] = full[modes // 2 :]


def from_modes(front_ref, back_ref, table_ref, lhs_ref):
    modes = 2 * front_ref.shape[0]
    cells, channels = lhs_ref.shape[:2]
    half = channels // 2
    lane = lax.broadcasted_iota(jnp.int32, (cells * SUB, LANES), 1)
    real = lane % (LANES // 2) < LANES // 4
    low_lane = lane < LANES // 2
    for block in range(half // SUB):
        rows = slice(SUB * block, SUB * (block + 1))
        values = jnp.concatenate([front_ref[:, 0, rows], back_ref[:, 0, rows]], axis=0)
        high, low = split(values.reshape(modes * SUB, LANES))
        full = dot(table_ref[0], jnp.concatenate([high, low], axis=1))
        full = full[:, :LANES] + full[:, LANES:] + dot(table_ref[1], high)
        plain, other = full[: cells * SUB], full[cells * SUB :]
        turned = jnp.where(
            real, -pltpu.roll(other, 3 * LANES // 4, 1), pltpu.roll(other, LANES // 4, 1)
        )
        inv = plain + turned
        swapped = pltpu.roll(inv, LANES // 2, 1)
        for at, doubled in (
            (0, jnp.where(low_lane, inv, swapped)),
            (half, jnp.where(low_lane, swapped, inv)),
        ):
            lhs_ref[:, at + SUB * block : at + SUB * (block + 1)] = doubled.reshape(
                cells, SUB, LANES
            )


def synthesise(lhs_ref, first, count, table_ref):
    values = lhs_ref[pl.ds(first, count)]
    high, low = split(values.reshape(-1, LANES))
    return dot(jnp.concatenate([high, low], axis=1), table_ref[...])


TAIL = (
    0.11650589762013625,
    0.06758867364360233,
    0.2686846227283619,
    -0.23671861048677273,
    0.38970758618179535,
    -0.10576817864886755,
)


def normal_parts(values):
    bell = jnp.exp(-0.5 * values * values)
    inner = 1.0 / (1.0 + 0.28 * jnp.abs(values))
    tail = TAIL[-1] * inner
    for factor in TAIL[-2::-1]:
        tail = (tail + factor) * inner
    tail = tail * bell
    return jnp.where(values >= 0.0, 1.0 - tail, tail), bell * (1.0 / math.sqrt(2.0 * math.pi))


def transpose_out(rows):
    parts = []
    for half in range(2):
        for part in range(2):
            shift = part * (LANES // 2) + half * (LANES // 4)
            parts.append(pltpu.roll(rows, LANES - shift, 1) if shift else rows)
    return jnp.concatenate(parts, axis=0).T[: LANES // 4]


def transpose_in(values):
    quarter = LANES // 4
    turned = jnp.concatenate([values] * 4, axis=0).T
    lane = lax.broadcasted_iota(jnp.int32, (quarter, LANES), 1) // quarter
    result = turned[:quarter]
    for half in range(2):
        for part in range(2):
            rows = turned[quarter * (2 * half + part) : quarter * (2 * half + part + 1)]
            result = jnp.where(lane == 2 * part + half, rows, result)
    return result


def turn_down(rows):
    lane = lax.broadcasted_iota(jnp.int32, rows.shape, 1) < LANES // 2
    rolled = pltpu.roll(rows, LANES // 2, 1)
    return jnp.where(lane, rolled, -rolled)


def spanwise_kernel(sizes, x_ref, table_ref, keep_ref, send_ref, down_ref, back_ref, coef_ref):
    step = pl.program_id(1)
    cells, _, channels, span = x_ref.shape

    @pl.when((step == 0) & (pl.program_id(0) == 0))
    def _():
        make_tables(down_ref, back_ref, *sizes)

    high, low = split(x_ref[...].reshape(cells * channels, span))
    analyse(high, low, table_ref, step * cells, coef_ref)

    @pl.when(step == pl.num_programs(1) - 1)
    def _():
        to_modes(coef_ref, down_ref, keep_ref, send_ref)


def pointwise_kernel(transposed, values_ref, local_ref, bias_ref, out_ref):
    weight = local_ref[...]
    channels = weight.shape[0]
    if transposed:
        weight = weight.T
    high, low = split(weight)
    lhs = jnp.concatenate([high, high, low], axis=1)
    if bias_ref is not None:
        row = jnp.broadcast_to(bias_ref[...], (channels, channels))
        column = row.T[:, :1]
    for cell in range(values_ref.shape[0]):
        high, low = split(values_ref[cell, 0])
        full = dot(lhs, jnp.concatenate([high, low, high], axis=0))
        out_ref[cell, 0] = full if bias_ref is None else full + column


def mix_kernel(*refs):
    *piece_refs, w_ref, modes_ref, mixed_ref, first_scr, second_scr = refs
    planes = modes_ref.shape[1]
    kz_count = w_ref.shape[1]
    quarter = LANES // 4
    for plane in range(planes):
        total = piece_refs[0][0, plane]
        for ref in piece_refs[1:]:
            total = total + ref[0, plane]
        modes_ref[0, plane] = total
        for kz in range(kz_count):
            sums = [None, None]
            for half in range(2):
                weight = w_ref[0, kz, quarter * half : quarter * (half + 1)]
                for part in range(2):
                    at = half * (LANES // 2) + part * quarter + kz
                    term = total[:, at : at + 1] * weight
                    sums[part] = term if sums[part] is None else sums[part] + term
            first_scr[kz : kz + 1] = jnp.sum(sums[0], axis=0, keepdims=True)
            second_scr[kz : kz + 1] = jnp.sum(sums[1], axis=0, keepdims=True)
        rows = first_scr[...] - turn_down(second_scr[...])
        mixed_ref[0, plane] = transpose_out(rows)


def middle_kernel(
    local_ref, up_ref, front_ref, back_ref, synth_ref, table_ref, down_ref, back_table_ref, *rest
):
    act_ref, dpre_ref, keep_ref, send_ref, lhs_ref, coef_ref = rest[-6:]
    step = pl.program_id(1)
    cells, _, channels, span = up_ref.shape

    @pl.when(step == 0)
    def _():
        from_modes(front_ref, back_ref, back_table_ref, lhs_ref)

    spectral = synthesise(lhs_ref, step * cells, cells, synth_ref)
    pre = spectral.reshape(cells, channels, span) + local_ref[:, 0]
    cumulative, density = normal_parts(pre)
    act_ref[:, 0] = pre * cumulative
    dpre = up_ref[:, 0] * (cumulative + pre * density)
    dpre_ref[:, 0] = dpre
    high, low = split(dpre.reshape(cells * channels, span))
    analyse(high, low, table_ref, step * cells, coef_ref)

    @pl.when(step == pl.num_programs(1) - 1)
    def _():
        to_modes(coef_ref, down_ref, keep_ref, send_ref)


def adjoint_kernel(*refs):
    *piece_refs, w_ref, dmixed_ref, dmodes_ref = refs
    planes = dmixed_ref.shape[1]
    kz_count, channels, width = w_ref.shape[1:]
    quarter = LANES // 4
    weight = w_ref[0].reshape(kz_count * channels, width)
    w_high, w_low = split(weight)
    lane = lax.broadcasted_iota(jnp.int32, (channels, LANES // 2), 1) % quarter
    for plane in range(planes):
        total = piece_refs[0][0, plane]
        for ref in piece_refs[1:]:
            total = total + ref[0, plane]
        dmixed_ref[0, plane] = total
        rows = transpose_in(total)
        both = jnp.concatenate([rows, turn_down(rows)], axis=0)
        high, low = split(both)
        right = jnp.concatenate([high, low], axis=0).T
        full = dot(w_high, right)
        full = full[:, : LANES // 2] + full[:, LANES // 2 :] + dot(w_low, right[:, : LANES // 2])
        full = full.reshape(kz_count, channels, LANES // 2)
        result = jnp.zeros((channels, LANES // 2), F32)
        for kz in range(kz_count):
            result = jnp.where(lane == kz, full[kz], result)
        dmodes_ref[0, plane] = jnp.concatenate(
            [result[: channels // 2], result[channels // 2 :]], axis=1
        )


def weight_grad_kernel(modes_ref, dmixed_ref, grad_ref, rows_scr):
    planes = modes_ref.shape[1]
    kz_count = grad_ref.shape[1]
    quarter = LANES // 4
    for plane in range(planes):
        rows = transpose_in(dmixed_ref[0, plane])
        rows_scr[2 * plane] = rows
        rows_scr[2 * plane + 1] = turn_down(rows)
    for kz in range(kz_count):
        for half in range(2):
            total = None
            for plane in range(planes):
                for part in range(2):
                    at = half * (LANES // 2) + part * quarter + kz
                    column = modes_ref[0, plane, :, at : at + 1]
                    term = column * rows_scr[2 * plane + part, kz : kz + 1]
                    total = term if total is None else total + term
            grad_ref[0, kz, quarter * half : quarter * (half + 1)] = total


def input_grad_kernel(local_ref, front_ref, back_ref, synth_ref, back_table_ref, *rest):
    out_ref, lhs_ref = rest[-2:]
    step = pl.program_id(1)
    cells, _, channels, span = local_ref.shape

    @pl.when(step == 0)
    def _():
        from_modes(front_ref, back_ref, back_table_ref, lhs_ref)

    spectral = synthesise(lhs_ref, step * cells, cells, synth_ref)
    out_ref[:, 0] = spectral.reshape(cells, channels, span) + local_ref[:, 0]


def swap(values, step):
    count = lax.axis_size("stream")
    return lax.ppermute(values, "stream", [(i, i ^ stage_mask(i, step)) for i in range(count)])


def beside(first, second):
    return lax.optimization_barrier((first, second))


def scatter_sum(keep, send, work):
    pieces = [keep, swap(send, 0)]
    half = keep.shape[0]
    done = None
    for step in range(1, len(stage_masks())):
        half //= 2
        part = pieces[0][half : 2 * half]
        for piece in pieces[1:]:
            part = part + piece[half : 2 * half]
        moved = swap(part, step)
        if step == 1:
            moved, done = beside(moved, work())
        pieces.append(moved)
    return pieces, done


def gather_all(values, work=None):
    done = None
    for step in reversed(range(1, len(stage_masks()))):
        moved = swap(values, step)
        if step == 1 and work is not None:
            moved, done = beside(moved, work())
        values = jnp.concatenate([values, moved], axis=0)
    return values, swap(values, 0), done


def params():
    return pltpu.CompilerParams(vmem_limit_bytes=VMEM_LIMIT)


def whole(array):
    rank = len(array.shape)
    return pl.BlockSpec(array.shape, lambda *_: (0,) * rank)


def per_device(snapshot, mode_weight, local_weight, offset_bias, upstream):
    cells, planes, span, channels = snapshot.shape
    owned, kz_count = mode_weight.shape[:2]
    total_modes = owned * lax.axis_size("stream")
    half_modes = total_modes // 2
    half_channels = channels // 2
    shape = jax.ShapeDtypeStruct
    x = jnp.swapaxes(snapshot, 2, 3)
    up = jnp.swapaxes(upstream, 2, 3)
    scale = float(cells * lax.axis_size("stream") * span)
    ana_fwd, ana_inv, syn_fwd, syn_inv = map(jnp.asarray, span_tables(span, kz_count, scale))
    step_cells = 4
    grid = (planes, cells // step_cells)
    coef_scr = pltpu.VMEM((half_channels // SUB, 2 * cells * SUB, LANES), F32)
    lhs_scr = pltpu.VMEM((cells, channels, LANES), F32)
    down = shape((2, total_modes * SUB, 2 * cells * SUB), BF16)
    back = shape((2, 2 * cells * SUB, total_modes * SUB), BF16)
    grid_block = pl.BlockSpec((step_cells, 1, channels, span), lambda p, s: (s, p, 0, 0))
    half_block = pl.BlockSpec((half_modes, 1, half_channels, LANES), lambda p, s: (0, p, 0, 0))
    own_block = pl.BlockSpec((1, planes, half_channels, LANES), lambda j: (j, 0, 0, 0))
    weight_block = pl.BlockSpec((1, kz_count, channels, 2 * channels), lambda j: (j, 0, 0, 0))
    own_shape = shape((owned, planes, half_channels, LANES), F32)
    half_shape = shape((half_modes, planes, half_channels, LANES), F32)
    grid_shape = shape(x.shape, F32)

    keep, send, down, back = pl.pallas_call(
        functools.partial(spanwise_kernel, (owned, total_modes, cells)),
        grid=grid,
        in_specs=[grid_block, whole(ana_fwd)],
        out_specs=[half_block, half_block, whole(down), whole(back)],
        out_shape=[half_shape, half_shape, down, back],
        scratch_shapes=[coef_scr],
        compiler_params=params(),
        name="spanwise",
    )(x, ana_fwd)

    def local_forward():
        return pl.pallas_call(
            functools.partial(pointwise_kernel, True),
            grid=grid,
            in_specs=[grid_block, whole(local_weight), whole(offset_bias[None])],
            out_specs=grid_block,
            out_shape=grid_shape,
            compiler_params=params(),
            name="local_forward",
        )(x, local_weight, offset_bias[None])

    pieces, local = scatter_sum(keep, send, local_forward)
    modes, mixed = pl.pallas_call(
        mix_kernel,
        grid=(owned,),
        in_specs=[own_block] * len(pieces) + [weight_block],
        out_specs=[own_block] * 2,
        out_shape=[own_shape] * 2,
        scratch_shapes=[pltpu.VMEM((kz_count, LANES), F32)] * 2,
        compiler_params=params(),
        name="mix",
    )(*pieces, mode_weight)
    front, behind, _ = gather_all(mixed)
    act, dpre, keep, send = pl.pallas_call(
        middle_kernel,
        grid=grid,
        in_specs=[
            grid_block, grid_block, half_block, half_block,
            whole(syn_inv), whole(ana_inv), whole(down), whole(back),
        ],
        out_specs=[grid_block, grid_block, half_block, half_block],
        out_shape=[grid_shape, grid_shape, half_shape, half_shape],
        scratch_shapes=[lhs_scr, coef_scr],
        compiler_params=params(),
        name="middle",
    )(local, up, front, behind, syn_inv, ana_inv, down, back)

    def local_backward():
        return pl.pallas_call(
            lambda values, weight, out: pointwise_kernel(False, values, weight, None, out),
            grid=grid,
            in_specs=[grid_block, whole(local_weight)],
            out_specs=grid_block,
            out_shape=grid_shape,
            compiler_params=params(),
            name="local_backward",
        )(dpre, local_weight)

    pieces, local = scatter_sum(keep, send, local_backward)
    dmixed, dmodes = pl.pallas_call(
        adjoint_kernel,
        grid=(owned,),
        in_specs=[own_block] * len(pieces) + [weight_block],
        out_specs=[own_block] * 2,
        out_shape=[own_shape] * 2,
        compiler_params=params(),
        name="adjoint",
    )(*pieces, mode_weight)

    def weight_grad():
        return pl.pallas_call(
            weight_grad_kernel,
            grid=(owned,),
            in_specs=[own_block] * 2,
            out_specs=weight_block,
            out_shape=shape(mode_weight.shape, F32),
            scratch_shapes=[pltpu.VMEM((2 * planes, kz_count, LANES), F32)],
            compiler_params=params(),
            name="weight_grad",
        )(modes, dmixed)

    front, behind, grad_modes = gather_all(dmodes, weight_grad)
    grad_snapshot = pl.pallas_call(
        input_grad_kernel,
        grid=grid,
        in_specs=[grid_block, half_block, half_block, whole(syn_fwd), whole(back)],
        out_specs=grid_block,
        out_shape=grid_shape,
        scratch_shapes=[lhs_scr],
        compiler_params=params(),
        name="input_grad",
    )(local, front, behind, syn_fwd, back)
    return jnp.swapaxes(act, 2, 3), jnp.swapaxes(grad_snapshot, 2, 3), grad_modes


def solution(mesh):
    wide = P("stream", "group", None, None)
    return jax.shard_map(
        per_device,
        mesh=mesh,
        in_specs=(wide, P("stream", None, None, None), P(), P(), wide),
        out_specs=(wide, wide, wide),
        check_vma=False,
    )
```

```python
import functools
import math

import jax
import jax.numpy as jnp
import numpy as np
from jax import lax
from jax.experimental import pallas as pl
from jax.experimental.pallas import tpu as pltpu
from jax.sharding import PartitionSpec as P

F32 = jnp.float32
BF16 = jnp.bfloat16
LANES = 128
SUB = 8
VMEM_LIMIT = 16 << 20
STEP = 8


def split_np(values):
    values = values.astype(np.float32)
    high = values.astype(BF16)
    low = (values - high.astype(np.float32)).astype(BF16)
    return high, low


def span_tables(length, modes, scale):
    angle = 2.0 * np.pi * (np.outer(np.arange(length), np.arange(modes)) % length) / length
    forward = np.concatenate([np.cos(angle), -np.sin(angle)], axis=1)
    factor = np.where(np.arange(modes) == 0, 1.0, 2.0) / scale
    backward = forward * np.concatenate([factor, factor])[None, :]

    def analysis(table):
        flipped = np.concatenate([table[:, modes:], -table[:, :modes]], axis=1)
        both = np.concatenate([table, flipped], axis=1)
        return np.concatenate(split_np(both), axis=1)

    def synthesis(table):
        high, low = split_np(table.T)
        return np.concatenate([high, low, high, np.zeros_like(high)], axis=0)

    return analysis(forward), analysis(backward), synthesis(forward), synthesis(backward)


def stage_masks():
    count = lax.axis_size("stream")
    bits = count.bit_length() - 1
    assert 1 << bits == count
    return [1] + [1 << i | 1 for i in range(1, bits)]


def stage_class(index):
    return (index ^ index >> 1 ^ index >> 2) & 1


def stage_mask(index, step):
    masks = stage_masks()
    if len(masks) > 2 and step in (1, 2) and stage_class(index):
        step = 3 - step
    return masks[step]


def mode_angles(position, inner, cell, owned, total_modes, cells):
    me = lax.axis_index("stream")
    masks = stage_masks()
    steps = len(masks)
    length = cells * (1 << steps)
    assert length & (length - 1) == 0
    bits = [position >> (steps - 1 - step) & 1 for step in range(steps)]
    if steps > 2:
        other = (bits[0] ^ stage_class(me)) & 1
        bits[1], bits[2] = (
            jnp.where(other == 1, bits[2], bits[1]),
            jnp.where(other == 1, bits[1], bits[2]),
        )
    block = jnp.zeros_like(position) + me
    for bit, mask in zip(bits, masks):
        block = block ^ bit * mask
    rows = block * owned + inner
    wave = jnp.where(rows < total_modes // 2, rows, rows - total_modes)
    phase = wave * (me * cells + cell) & (length - 1)
    phase = jnp.where(phase > length // 2, phase - length, phase)
    return phase.astype(F32) * (2.0 * math.pi / length)


def split(values):
    high = values.astype(BF16)
    return high, (values - high.astype(F32)).astype(BF16)


def dot(left, right):
    return jnp.dot(left, right, preferred_element_type=F32)


def make_tables(down_ref, back_ref, owned, total_modes, cells):
    def iota(shape, axis):
        return lax.broadcasted_iota(jnp.int32, shape, axis)

    def expand(table, ref):
        rows, lanes = table.shape
        full = jnp.broadcast_to(table[:, None, :], (rows, SUB, lanes)).reshape(rows * SUB, lanes)
        same = (iota(full.shape, 0) & (SUB - 1)) == (iota(full.shape, 1) & (SUB - 1))
        high, low = split(jnp.where(same, full, 0.0))
        ref[0] = high
        ref[1] = low

    def table(shape, mode_axis):
        mode = iota(shape, mode_axis)
        cell = iota(shape, 1 - mode_axis)
        if mode_axis == 1:
            mode = mode >> 3
        else:
            cell = cell >> 3
        shift = owned.bit_length() - 1
        angles = mode_angles(
            mode >> shift, mode & (owned - 1), cell & (cells - 1), owned, total_modes, cells
        )
        return jnp.where(cell < cells, jnp.cos(angles), jnp.sin(angles))

    expand(table((total_modes, 2 * cells * SUB), 0), down_ref)
    expand(table((2 * cells, total_modes * SUB), 1), back_ref)


def analyse(values_high, values_low, table_ref, at, coef_ref):
    full = dot(values_high, table_ref[...])
    full = full[:, :LANES] + full[:, LANES:] + dot(values_low, table_ref[:, :LANES])
    cells = coef_ref.shape[1] // (2 * SUB)
    half = 4 * SUB
    low_lane = lax.broadcasted_iota(jnp.int32, (half, LANES), 1) < LANES // 2
    for i in range(full.shape[0] // (2 * half)):
        low = full[2 * half * i : 2 * half * i + half]
        high = full[2 * half * i + half : 2 * half * (i + 1)]
        plain = jnp.where(low_lane, low, pltpu.roll(high, LANES // 2, 1))
        flipped = jnp.where(low_lane, pltpu.roll(low, LANES // 2, 1), high)
        for block in range(half // SUB):
            rows = slice(SUB * block, SUB * (block + 1))
            coef_ref[block, pl.ds((at + i) * SUB, SUB)] = plain[rows]
            coef_ref[block, pl.ds((cells + at + i) * SUB, SUB)] = flipped[rows]


def to_modes(coef_ref, table_ref, keep_ref, send_ref, plane):
    modes = 2 * keep_ref.shape[0]
    for block in range(coef_ref.shape[0]):
        high, low = split(coef_ref[block])
        full = dot(table_ref[0], jnp.concatenate([high, low], axis=1))
        full = full[:, :LANES] + full[:, LANES:] + dot(table_ref[1], high)
        full = full.reshape(modes, SUB, LANES)
        rows = slice(SUB * block, SUB * (block + 1))
        keep_ref[:, plane, rows] = full[: modes // 2]
        send_ref[:, plane, rows] = full[modes // 2 :]


def from_modes(front_ref, back_ref, table_ref, lhs_ref, plane):
    modes = 2 * front_ref.shape[0]
    cells, channels = lhs_ref.shape[:2]
    half = channels // 2
    lane = lax.broadcasted_iota(jnp.int32, (cells * SUB, LANES), 1)
    real = lane % (LANES // 2) < LANES // 4
    low_lane = lane < LANES // 2
    for block in range(half // SUB):
        rows = slice(SUB * block, SUB * (block + 1))
        values = jnp.concatenate([front_ref[:, plane, rows], back_ref[:, plane, rows]], axis=0)
        high, low = split(values.reshape(modes * SUB, LANES))
        full = dot(table_ref[0], jnp.concatenate([high, low], axis=1))
        full = full[:, :LANES] + full[:, LANES:] + dot(table_ref[1], high)
        plain, other = full[: cells * SUB], full[cells * SUB :]
        turned = jnp.where(
            real, -pltpu.roll(other, 3 * LANES // 4, 1), pltpu.roll(other, LANES // 4, 1)
        )
        inv = plain + turned
        swapped = pltpu.roll(inv, LANES // 2, 1)
        for at, doubled in (
            (0, jnp.where(low_lane, inv, swapped)),
            (half, jnp.where(low_lane, swapped, inv)),
        ):
            lhs_ref[:, at + SUB * block : at + SUB * (block + 1)] = doubled.reshape(
                cells, SUB, LANES
            )


def synthesise(lhs_ref, first, count, table_ref):
    values = lhs_ref[pl.ds(first, count)]
    high, low = split(values.reshape(-1, LANES))
    return dot(jnp.concatenate([high, low], axis=1), table_ref[...])


TAIL = (
    0.11650589762013625,
    0.06758867364360233,
    0.2686846227283619,
    -0.23671861048677273,
    0.38970758618179535,
    -0.10576817864886755,
)


def normal_parts(values):
    bell = jnp.exp(-0.5 * values * values)
    inner = 1.0 / (1.0 + 0.28 * jnp.abs(values))
    tail = TAIL[-1] * inner
    for factor in TAIL[-2::-1]:
        tail = (tail + factor) * inner
    tail = tail * bell
    return jnp.where(values >= 0.0, 1.0 - tail, tail), bell * (1.0 / math.sqrt(2.0 * math.pi))


def transpose_out(rows):
    parts = []
    for half in range(2):
        for part in range(2):
            shift = part * (LANES // 2) + half * (LANES // 4)
            parts.append(pltpu.roll(rows, LANES - shift, 1) if shift else rows)
    return jnp.concatenate(parts, axis=0).T[: LANES // 4]


def transpose_in(values):
    quarter = LANES // 4
    turned = jnp.concatenate([values] * 4, axis=0).T
    lane = lax.broadcasted_iota(jnp.int32, (quarter, LANES), 1) // quarter
    result = turned[:quarter]
    for half in range(2):
        for part in range(2):
            rows = turned[quarter * (2 * half + part) : quarter * (2 * half + part + 1)]
            result = jnp.where(lane == 2 * part + half, rows, result)
    return result


def turn_down(rows):
    lane = lax.broadcasted_iota(jnp.int32, rows.shape, 1) < LANES // 2
    rolled = pltpu.roll(rows, LANES // 2, 1)
    return jnp.where(lane, rolled, -rolled)


def chunks(cells, planes):
    return [(p, at) for p in range(planes) for at in range(0, cells, STEP)]


def spanwise_kernel(
    sizes, x_ref, table_hbm, keep_ref, send_ref, down_ref, back_ref,
    table_ref, x_scr, coef_ref, sems,
):
    cells, planes, channels, span = x_ref.shape
    work = chunks(cells, planes)
    copies = [
        pltpu.make_async_copy(x_ref.at[pl.ds(at, STEP), p], x_scr.at[i], sems.at[i])
        for i, (p, at) in enumerate(work)
    ]
    copies.append(pltpu.make_async_copy(table_hbm, table_ref, sems.at[len(work)]))
    for copy in copies[-1:] + copies[:-1]:
        copy.start()
    make_tables(down_ref, back_ref, *sizes)
    copies[-1].wait()
    for i, (p, at) in enumerate(work):
        copies[i].wait()
        high, low = split(x_scr[i].reshape(STEP * channels, span))
        analyse(high, low, table_ref, at, coef_ref.at[p])
    for p in range(planes):
        to_modes(coef_ref.at[p], down_ref, keep_ref, send_ref, p)


def pointwise_kernel(transposed, values_ref, local_ref, bias_ref, out_ref):
    weight = local_ref[...]
    channels = weight.shape[0]
    if transposed:
        weight = weight.T
    high, low = split(weight)
    lhs = jnp.concatenate([high, high, low], axis=1)
    if bias_ref is not None:
        row = jnp.broadcast_to(bias_ref[...], (channels, channels))
        column = row.T[:, :1]
    cells, planes = values_ref.shape[:2]

    def body(step, _):
        for p in range(planes):
            for cell in range(2):
                at = 2 * step + cell
                high, low = split(values_ref[at, p])
                full = dot(lhs, jnp.concatenate([high, low, high], axis=0))
                out_ref[at, p] = full if bias_ref is None else full + column
        return 0

    lax.fori_loop(0, cells // 2, body, 0)


def total_of(piece_refs, j, plane):
    total = piece_refs[0][j, plane]
    for ref in piece_refs[1:]:
        total = total + ref[j, plane]
    return total


def mix_kernel(*refs):
    *piece_refs, w_ref, modes_ref, mixed_ref = refs
    owned, planes = modes_ref.shape[:2]
    kz_count, channels = w_ref.shape[1:3]
    wide = SUB * channels
    low_lane = lax.broadcasted_iota(jnp.int32, (kz_count, LANES), 1) < channels
    row = lax.broadcasted_iota(jnp.int32, (kz_count, wide), 0) & (SUB - 1)
    own = lax.broadcasted_iota(jnp.int32, (kz_count, wide), 1) // channels == row

    def body(j, _):
        sides = []
        for plane in range(planes):
            total = total_of(piece_refs, j, plane)
            modes_ref[j, plane] = total
            rows = transpose_in(total)
            rolled = pltpu.roll(rows, channels, 1)
            for doubled in (jnp.where(low_lane, rows, rolled), jnp.where(low_lane, rolled, rows)):
                tiled = jnp.concatenate([doubled] * (wide // LANES), axis=1)
                sides.append(jnp.where(own, tiled, 0.0))
        results = []
        for at in range(0, kz_count, SUB):
            left = jnp.concatenate([side[at : at + SUB] for side in sides], axis=0)
            left = jnp.concatenate(split(left), axis=0)
            right = w_ref[j, at : at + SUB].reshape(wide, LANES)
            full = dot(left, jnp.concatenate(split(right), axis=1))
            count = full.shape[0] // 2
            full = full[:count, :LANES] + full[:count, LANES:] + full[count:, :LANES]
            results.append(full.reshape(planes, 2, SUB, LANES))
        for plane in range(planes):
            first, second = (
                jnp.concatenate([result[plane, part] for result in results], axis=0)
                for part in range(2)
            )
            mixed_ref[j, plane] = transpose_out(first - turn_down(second))
        return 0

    lax.fori_loop(0, owned, body, 0)


def middle_kernel(
    local_ref, up_ref, front_ref, back_ref, synth_ref, table_ref, down_ref, back_table_ref,
    act_ref, dpre_ref, keep_ref, send_ref, lhs_ref, coef_ref,
):
    cells, planes, channels, span = up_ref.shape
    for p in range(planes):
        from_modes(front_ref, back_ref, back_table_ref, lhs_ref.at[p], p)
    for p, at in chunks(cells, planes):
        rows = pl.ds(at, STEP)
        spectral = synthesise(lhs_ref.at[p], at, STEP, synth_ref)
        pre = spectral.reshape(STEP, channels, span) + local_ref[rows, p]
        cumulative, density = normal_parts(pre)
        act_ref[rows, p] = pre * cumulative
        dpre = up_ref[rows, p] * (cumulative + pre * density)
        dpre_ref[rows, p] = dpre
        high, low = split(dpre.reshape(STEP * channels, span))
        analyse(high, low, table_ref, at, coef_ref.at[p])
    for p in range(planes):
        to_modes(coef_ref.at[p], down_ref, keep_ref, send_ref, p)


def adjoint_kernel(*refs):
    *piece_refs, w_ref, dmixed_ref, dmodes_ref = refs
    owned, planes = dmixed_ref.shape[:2]
    kz_count, channels, width = w_ref.shape[1:]
    quarter = LANES // 4
    lane = lax.broadcasted_iota(jnp.int32, (channels, LANES // 2), 1) % quarter

    def body(j, _):
        w_high, w_low = split(w_ref[j].reshape(kz_count * channels, width))
        for plane in range(planes):
            total = total_of(piece_refs, j, plane)
            dmixed_ref[j, plane] = total
            rows = transpose_in(total)
            both = jnp.concatenate([rows, turn_down(rows)], axis=0)
            high, low = split(both)
            right = jnp.concatenate([high, low], axis=0).T
            full = dot(w_high, right)
            full = (
                full[:, : LANES // 2] + full[:, LANES // 2 :] + dot(w_low, right[:, : LANES // 2])
            )
            full = full.reshape(kz_count, channels, LANES // 2)
            result = jnp.zeros((channels, LANES // 2), F32)
            for kz in range(kz_count):
                result = jnp.where(lane == kz, full[kz], result)
            dmodes_ref[j, plane] = jnp.concatenate(
                [result[: channels // 2], result[channels // 2 :]], axis=1
            )
        return 0

    lax.fori_loop(0, owned, body, 0)


def weight_grad_kernel(modes_ref, dmixed_ref, grad_ref):
    owned, planes = modes_ref.shape[:2]
    kz_count, channels = grad_ref.shape[1:3]
    assert planes * channels == LANES
    half = channels // 2
    low_lane = lax.broadcasted_iota(jnp.int32, (half, LANES), 1) < channels
    lane = lax.broadcasted_iota(jnp.int32, (2 * channels, LANES), 1) & (kz_count - 1)

    def body(j, _):
        right = []
        for plane in range(planes):
            rows = transpose_in(dmixed_ref[j, plane])
            right += [rows, turn_down(rows)]
        right = jnp.concatenate(split(jnp.concatenate(right, axis=0)), axis=1)
        first, second = modes_ref[j, 0], modes_ref[j, 1]
        left = jnp.concatenate(
            [
                jnp.where(low_lane, first, pltpu.roll(second, channels, 1)),
                jnp.where(low_lane, pltpu.roll(first, channels, 1), second),
            ],
            axis=0,
        )
        left = jnp.concatenate(split(left), axis=0)
        for kz in range(kz_count):
            full = dot(jnp.where(lane == kz, left, jnp.zeros_like(left)), right)
            grad_ref[j, kz] = (
                full[:channels, :LANES] + full[:channels, LANES:] + full[channels:, :LANES]
            )
        return 0

    lax.fori_loop(0, owned, body, 0)


def input_grad_kernel(
    local_ref, front_ref, back_ref, synth_ref, back_table_ref, out_ref, out_scr, lhs_ref, sems
):
    cells, planes, channels, span = local_ref.shape
    copies = []
    for i, (p, at) in enumerate(chunks(cells, planes)):
        if at == 0:
            from_modes(front_ref, back_ref, back_table_ref, lhs_ref.at[p], p)
        rows = pl.ds(at, STEP)
        spectral = synthesise(lhs_ref.at[p], at, STEP, synth_ref)
        out_scr[i] = spectral.reshape(STEP, channels, span) + local_ref[rows, p]
        copies.append(pltpu.make_async_copy(out_scr.at[i], out_ref.at[rows, p], sems.at[i]))
        copies[-1].start()
    for copy in copies:
        copy.wait()


def swap(values, step):
    count = lax.axis_size("stream")
    return lax.ppermute(values, "stream", [(i, i ^ stage_mask(i, step)) for i in range(count)])


def beside(first, second):
    return lax.optimization_barrier((first, second))


def scatter_sum(keep, send, work):
    pieces = [keep, swap(send, 0)]
    half = keep.shape[0]
    done = None
    for step in range(1, len(stage_masks())):
        half //= 2
        part = pieces[0][half : 2 * half]
        for piece in pieces[1:]:
            part = part + piece[half : 2 * half]
        moved = swap(part, step)
        if step == 1:
            moved, done = beside(moved, work())
        pieces.append(moved)
    return pieces, done


def gather_all(values, work=None):
    done = None
    for step in reversed(range(1, len(stage_masks()))):
        moved = swap(values, step)
        if step == 1 and work is not None:
            moved, done = beside(moved, work())
        values = jnp.concatenate([values, moved], axis=0)
    return values, swap(values, 0), done


def params():
    return pltpu.CompilerParams(vmem_limit_bytes=VMEM_LIMIT)


def whole(array):
    rank = len(array.shape)
    return pl.BlockSpec(array.shape, lambda *_: (0,) * rank)


def per_device(snapshot, mode_weight, local_weight, offset_bias, upstream):
    cells, planes, span, channels = snapshot.shape
    owned, kz_count = mode_weight.shape[:2]
    total_modes = owned * lax.axis_size("stream")
    half_modes = total_modes // 2
    half_channels = channels // 2
    shape = jax.ShapeDtypeStruct
    x = jnp.swapaxes(snapshot, 2, 3)
    up = jnp.swapaxes(upstream, 2, 3)
    scale = float(cells * lax.axis_size("stream") * span)
    ana_fwd, ana_inv, syn_fwd, syn_inv = map(jnp.asarray, span_tables(span, kz_count, scale))
    pieces_of = len(chunks(cells, planes))
    coef_scr = pltpu.VMEM((planes, half_channels // SUB, 2 * cells * SUB, LANES), F32)
    lhs_scr = pltpu.VMEM((planes, cells, channels, LANES), F32)
    span_scr = pltpu.VMEM((pieces_of, STEP, channels, span), F32)
    sem_scr = pltpu.SemaphoreType.DMA((pieces_of + 1,))
    down = shape((2, total_modes * SUB, 2 * cells * SUB), BF16)
    back = shape((2, 2 * cells * SUB, total_modes * SUB), BF16)
    here = pl.BlockSpec(memory_space=pltpu.VMEM)
    apart = pl.BlockSpec(memory_space=pl.ANY)
    own_shape = shape((owned, planes, half_channels, LANES), F32)
    half_shape = shape((half_modes, planes, half_channels, LANES), F32)
    grid_shape = shape(x.shape, F32)

    keep, send, down, back = pl.pallas_call(
        functools.partial(spanwise_kernel, (owned, total_modes, cells)),
        in_specs=[apart, apart],
        out_specs=[here] * 4,
        out_shape=[half_shape, half_shape, down, back],
        scratch_shapes=[pltpu.VMEM(ana_fwd.shape, BF16), span_scr, coef_scr, sem_scr],
        compiler_params=params(),
        name="spanwise",
    )(pltpu.with_memory_space_constraint(x, pltpu.HBM), pltpu.with_memory_space_constraint(ana_fwd, pltpu.HBM))

    def local_forward():
        return pl.pallas_call(
            functools.partial(pointwise_kernel, True),
            in_specs=[here] * 3,
            out_specs=here,
            out_shape=grid_shape,
            compiler_params=params(),
            name="local_forward",
        )(x, local_weight, offset_bias[None])

    pieces, local = scatter_sum(keep, send, local_forward)
    modes, mixed = pl.pallas_call(
        mix_kernel,
        in_specs=[here] * (len(pieces) + 1),
        out_specs=[here] * 2,
        out_shape=[own_shape] * 2,
        compiler_params=params(),
        name="mix",
    )(*pieces, mode_weight)
    front, behind, _ = gather_all(mixed)
    act, dpre, keep, send = pl.pallas_call(
        middle_kernel,
        in_specs=[here] * 8,
        out_specs=[here] * 4,
        out_shape=[grid_shape, grid_shape, half_shape, half_shape],
        scratch_shapes=[lhs_scr, coef_scr],
        compiler_params=params(),
        name="middle",
    )(local, up, front, behind, syn_inv, ana_inv, down, back)

    def local_backward():
        return pl.pallas_call(
            lambda values, weight, out: pointwise_kernel(False, values, weight, None, out),
            in_specs=[here] * 2,
            out_specs=here,
            out_shape=grid_shape,
            compiler_params=params(),
            name="local_backward",
        )(dpre, local_weight)

    pieces, local = scatter_sum(keep, send, local_backward)
    dmixed, dmodes = pl.pallas_call(
        adjoint_kernel,
        in_specs=[here] * (len(pieces) + 1),
        out_specs=[here] * 2,
        out_shape=[own_shape] * 2,
        compiler_params=params(),
        name="adjoint",
    )(*pieces, mode_weight)

    def weight_grad():
        return pl.pallas_call(
            weight_grad_kernel,
            in_specs=[here] * 2,
            out_specs=here,
            out_shape=shape(mode_weight.shape, F32),
            compiler_params=params(),
            name="weight_grad",
        )(modes, dmixed)

    front, behind, grad_modes = gather_all(dmodes, weight_grad)
    grad_snapshot = pl.pallas_call(
        input_grad_kernel,
        in_specs=[here] * 5,
        out_specs=apart,
        out_shape=grid_shape,
        scratch_shapes=[span_scr, lhs_scr, sem_scr],
        compiler_params=params(),
        name="input_grad",
    )(local, front, behind, syn_fwd, back)
    return jnp.swapaxes(act, 2, 3), jnp.swapaxes(grad_snapshot, 2, 3), grad_modes


def solution(mesh):
    wide = P("stream", "group", None, None)
    return jax.shard_map(
        per_device,
        mesh=mesh,
        in_specs=(wide, P("stream", None, None, None), P(), P(), wide),
        out_specs=(wide, wide, wide),
        check_vma=False,
    )
```

```python
import functools
import math

import jax
import jax.numpy as jnp
import numpy as np
from jax import lax
from jax.experimental import pallas as pl
from jax.experimental.pallas import tpu as pltpu
from jax.sharding import PartitionSpec as P

F32 = jnp.float32
BF16 = jnp.bfloat16
LANES = 128
SUB = 8
VMEM_LIMIT = 16 << 20
STEP = 8


def split_np(values):
    values = values.astype(np.float32)
    high = values.astype(BF16)
    low = (values - high.astype(np.float32)).astype(BF16)
    return high, low


def span_tables(length, modes, scale):
    angle = 2.0 * np.pi * (np.outer(np.arange(length), np.arange(modes)) % length) / length
    forward = np.concatenate([np.cos(angle), -np.sin(angle)], axis=1)
    factor = np.where(np.arange(modes) == 0, 1.0, 2.0) / scale
    backward = forward * np.concatenate([factor, factor])[None, :]

    def analysis(table):
        flipped = np.concatenate([table[:, modes:], -table[:, :modes]], axis=1)
        both = np.concatenate([table, flipped], axis=1)
        return np.concatenate(split_np(both), axis=1)

    def synthesis(table):
        high, low = split_np(table.T)
        return np.concatenate([high, low, high, np.zeros_like(high)], axis=0)

    return analysis(forward), analysis(backward), synthesis(forward), synthesis(backward)


def stage_masks():
    count = lax.axis_size("stream")
    bits = count.bit_length() - 1
    assert 1 << bits == count and bits >= 3
    return [1, 4, 2] + [1 << i for i in range(3, bits)]


def mode_angles(position, inner, cell, owned, total_modes, cells):
    me = lax.axis_index("stream")
    masks = stage_masks()
    steps = len(masks)
    length = cells * (1 << steps)
    assert length & (length - 1) == 0
    bits = [position >> (steps - 1 - step) & 1 for step in range(steps)]
    block = jnp.zeros_like(position) + me
    for bit, mask in zip(bits, masks):
        block = block ^ bit * mask
    rows = block * owned + inner
    wave = jnp.where(rows < total_modes // 2, rows, rows - total_modes)
    phase = wave * (me * cells + cell) & (length - 1)
    phase = jnp.where(phase > length // 2, phase - length, phase)
    return phase.astype(F32) * (2.0 * math.pi / length)


def split(values):
    high = values.astype(BF16)
    return high, (values - high.astype(F32)).astype(BF16)


def dot(left, right):
    return jnp.dot(left, right, preferred_element_type=F32)


def make_tables(down_ref, back_ref, owned, total_modes, cells):
    def iota(shape, axis):
        return lax.broadcasted_iota(jnp.int32, shape, axis)

    def expand(table, ref):
        rows, lanes = table.shape
        full = jnp.broadcast_to(table[:, None, :], (rows, SUB, lanes)).reshape(rows * SUB, lanes)
        same = (iota(full.shape, 0) & (SUB - 1)) == (iota(full.shape, 1) & (SUB - 1))
        high, low = split(jnp.where(same, full, 0.0))
        ref[0] = high
        ref[1] = low

    def table(shape, mode_axis):
        mode = iota(shape, mode_axis)
        cell = iota(shape, 1 - mode_axis)
        if mode_axis == 1:
            mode = mode >> 3
        else:
            cell = cell >> 3
        shift = owned.bit_length() - 1
        angles = mode_angles(
            mode >> shift, mode & (owned - 1), cell & (cells - 1), owned, total_modes, cells
        )
        return jnp.where(cell < cells, jnp.cos(angles), jnp.sin(angles))

    expand(table((total_modes, 2 * cells * SUB), 0), down_ref)
    expand(table((2 * cells, total_modes * SUB), 1), back_ref)


def analyse(values_high, values_low, table_ref, at, coef_ref):
    full = dot(values_high, table_ref[...])
    full = full[:, :LANES] + full[:, LANES:] + dot(values_low, table_ref[:, :LANES])
    cells = coef_ref.shape[1] // (2 * SUB)
    half = 4 * SUB
    low_lane = lax.broadcasted_iota(jnp.int32, (half, LANES), 1) < LANES // 2
    for i in range(full.shape[0] // (2 * half)):
        low = full[2 * half * i : 2 * half * i + half]
        high = full[2 * half * i + half : 2 * half * (i + 1)]
        plain = jnp.where(low_lane, low, pltpu.roll(high, LANES // 2, 1))
        flipped = jnp.where(low_lane, pltpu.roll(low, LANES // 2, 1), high)
        for block in range(half // SUB):
            rows = slice(SUB * block, SUB * (block + 1))
            coef_ref[block, pl.ds((at + i) * SUB, SUB)] = plain[rows]
            coef_ref[block, pl.ds((cells + at + i) * SUB, SUB)] = flipped[rows]


def to_modes(coef_ref, table_ref, keep_ref, send_ref, plane):
    modes = 2 * keep_ref.shape[0]
    for block in range(coef_ref.shape[0]):
        high, low = split(coef_ref[block])
        full = dot(table_ref[0], jnp.concatenate([high, low], axis=1))
        full = full[:, :LANES] + full[:, LANES:] + dot(table_ref[1], high)
        full = full.reshape(modes, SUB, LANES)
        rows = slice(SUB * block, SUB * (block + 1))
        keep_ref[:, plane, rows] = full[: modes // 2]
        send_ref[:, plane, rows] = full[modes // 2 :]


def from_modes(front_ref, back_ref, table_ref, lhs_ref, plane):
    modes = 2 * front_ref.shape[0]
    cells, channels = lhs_ref.shape[:2]
    half = channels // 2
    lane = lax.broadcasted_iota(jnp.int32, (cells * SUB, LANES), 1)
    real = lane % (LANES // 2) < LANES // 4
    low_lane = lane < LANES // 2
    for block in range(half // SUB):
        rows = slice(SUB * block, SUB * (block + 1))
        values = jnp.concatenate([front_ref[:, plane, rows], back_ref[:, plane, rows]], axis=0)
        high, low = split(values.reshape(modes * SUB, LANES))
        full = dot(table_ref[0], jnp.concatenate([high, low], axis=1))
        full = full[:, :LANES] + full[:, LANES:] + dot(table_ref[1], high)
        plain, other = full[: cells * SUB], full[cells * SUB :]
        turned = jnp.where(
            real, -pltpu.roll(other, 3 * LANES // 4, 1), pltpu.roll(other, LANES // 4, 1)
        )
        inv = plain + turned
        swapped = pltpu.roll(inv, LANES // 2, 1)
        for at, doubled in (
            (0, jnp.where(low_lane, inv, swapped)),
            (half, jnp.where(low_lane, swapped, inv)),
        ):
            lhs_ref[:, at + SUB * block : at + SUB * (block + 1)] = doubled.reshape(
                cells, SUB, LANES
            )


def synthesise(lhs_ref, first, count, table_ref):
    values = lhs_ref[pl.ds(first, count)]
    high, low = split(values.reshape(-1, LANES))
    return dot(jnp.concatenate([high, low], axis=1), table_ref[...])


TAIL = (
    0.11650589762013625,
    0.06758867364360233,
    0.2686846227283619,
    -0.23671861048677273,
    0.38970758618179535,
    -0.10576817864886755,
)


def normal_parts(values):
    bell = jnp.exp(-0.5 * values * values)
    inner = 1.0 / (1.0 + 0.28 * jnp.abs(values))
    tail = TAIL[-1] * inner
    for factor in TAIL[-2::-1]:
        tail = (tail + factor) * inner
    tail = tail * bell
    return jnp.where(values >= 0.0, 1.0 - tail, tail), bell * (1.0 / math.sqrt(2.0 * math.pi))


def transpose_out(rows):
    parts = []
    for half in range(2):
        for part in range(2):
            shift = part * (LANES // 2) + half * (LANES // 4)
            parts.append(pltpu.roll(rows, LANES - shift, 1) if shift else rows)
    return jnp.concatenate(parts, axis=0).T[: LANES // 4]


def transpose_in(values):
    quarter = LANES // 4
    turned = jnp.concatenate([values] * 4, axis=0).T
    lane = lax.broadcasted_iota(jnp.int32, (quarter, LANES), 1) // quarter
    result = turned[:quarter]
    for half in range(2):
        for part in range(2):
            rows = turned[quarter * (2 * half + part) : quarter * (2 * half + part + 1)]
            result = jnp.where(lane == 2 * part + half, rows, result)
    return result


def turn_down(rows):
    lane = lax.broadcasted_iota(jnp.int32, rows.shape, 1) < LANES // 2
    rolled = pltpu.roll(rows, LANES // 2, 1)
    return jnp.where(lane, rolled, -rolled)


def chunks(cells, planes):
    return [(p, at) for p in range(planes) for at in range(0, cells, STEP)]


def spanwise_kernel(
    sizes, x_ref, table_hbm, keep_ref, send_ref, down_ref, back_ref,
    table_ref, x_scr, coef_ref, sems,
):
    cells, planes, channels, span = x_ref.shape
    work = chunks(cells, planes)
    copies = [
        pltpu.make_async_copy(x_ref.at[pl.ds(at, STEP), p], x_scr.at[i], sems.at[i])
        for i, (p, at) in enumerate(work)
    ]
    copies.append(pltpu.make_async_copy(table_hbm, table_ref, sems.at[len(work)]))
    for copy in copies[-1:] + copies[:-1]:
        copy.start()
    make_tables(down_ref, back_ref, *sizes)
    copies[-1].wait()
    for i, (p, at) in enumerate(work):
        copies[i].wait()
        high, low = split(x_scr[i].reshape(STEP * channels, span))
        analyse(high, low, table_ref, at, coef_ref.at[p])
    for p in range(planes):
        to_modes(coef_ref.at[p], down_ref, keep_ref, send_ref, p)


def pointwise_kernel(transposed, values_ref, local_ref, bias_ref, out_ref):
    weight = local_ref[...]
    channels = weight.shape[0]
    if transposed:
        weight = weight.T
    high, low = split(weight)
    lhs = jnp.concatenate([high, high, low], axis=1)
    if bias_ref is not None:
        row = jnp.broadcast_to(bias_ref[...], (channels, channels))
        column = row.T[:, :1]
    cells, planes = values_ref.shape[:2]

    def body(step, _):
        for p in range(planes):
            for cell in range(2):
                at = 2 * step + cell
                high, low = split(values_ref[at, p])
                full = dot(lhs, jnp.concatenate([high, low, high], axis=0))
                out_ref[at, p] = full if bias_ref is None else full + column
        return 0

    lax.fori_loop(0, cells // 2, body, 0)


def total_of(piece_refs, j, plane):
    total = piece_refs[0][j, plane]
    for ref in piece_refs[1:]:
        total = total + ref[j, plane]
    return total


def mix_kernel(*refs):
    *piece_refs, w_ref, modes_ref, mixed_ref = refs
    owned, planes = modes_ref.shape[:2]
    kz_count, channels = w_ref.shape[1:3]
    wide = SUB * channels
    low_lane = lax.broadcasted_iota(jnp.int32, (kz_count, LANES), 1) < channels
    row = lax.broadcasted_iota(jnp.int32, (kz_count, wide), 0) & (SUB - 1)
    own = lax.broadcasted_iota(jnp.int32, (kz_count, wide), 1) // channels == row

    def body(j, _):
        sides = []
        for plane in range(planes):
            total = total_of(piece_refs, j, plane)
            modes_ref[j, plane] = total
            rows = transpose_in(total)
            rolled = pltpu.roll(rows, channels, 1)
            for doubled in (jnp.where(low_lane, rows, rolled), jnp.where(low_lane, rolled, rows)):
                tiled = jnp.concatenate([doubled] * (wide // LANES), axis=1)
                sides.append(jnp.where(own, tiled, 0.0))
        results = []
        for at in range(0, kz_count, SUB):
            left = jnp.concatenate([side[at : at + SUB] for side in sides], axis=0)
            left = jnp.concatenate(split(left), axis=0)
            right = w_ref[j, at : at + SUB].reshape(wide, LANES)
            full = dot(left, jnp.concatenate(split(right), axis=1))
            count = full.shape[0] // 2
            full = full[:count, :LANES] + full[:count, LANES:] + full[count:, :LANES]
            results.append(full.reshape(planes, 2, SUB, LANES))
        for plane in range(planes):
            first, second = (
                jnp.concatenate([result[plane, part] for result in results], axis=0)
                for part in range(2)
            )
            mixed_ref[j, plane] = transpose_out(first - turn_down(second))
        return 0

    lax.fori_loop(0, owned, body, 0)


def middle_kernel(
    local_ref, up_ref, front_ref, back_ref, synth_ref, table_ref, down_ref, back_table_ref,
    act_ref, dpre_ref, keep_ref, send_ref, lhs_ref, coef_ref,
):
    cells, planes, channels, span = up_ref.shape
    for p in range(planes):
        from_modes(front_ref, back_ref, back_table_ref, lhs_ref.at[p], p)
    for p, at in chunks(cells, planes):
        rows = pl.ds(at, STEP)
        spectral = synthesise(lhs_ref.at[p], at, STEP, synth_ref)
        pre = spectral.reshape(STEP, channels, span) + local_ref[rows, p]
        cumulative, density = normal_parts(pre)
        act_ref[rows, p] = pre * cumulative
        dpre = up_ref[rows, p] * (cumulative + pre * density)
        dpre_ref[rows, p] = dpre
        high, low = split(dpre.reshape(STEP * channels, span))
        analyse(high, low, table_ref, at, coef_ref.at[p])
    for p in range(planes):
        to_modes(coef_ref.at[p], down_ref, keep_ref, send_ref, p)


def adjoint_kernel(*refs):
    *piece_refs, w_ref, dmixed_ref, dmodes_ref = refs
    owned, planes = dmixed_ref.shape[:2]
    kz_count, channels, width = w_ref.shape[1:]
    quarter = LANES // 4
    lane = lax.broadcasted_iota(jnp.int32, (channels, LANES // 2), 1) % quarter

    def body(j, _):
        w_high, w_low = split(w_ref[j].reshape(kz_count * channels, width))
        for plane in range(planes):
            total = total_of(piece_refs, j, plane)
            dmixed_ref[j, plane] = total
            rows = transpose_in(total)
            both = jnp.concatenate([rows, turn_down(rows)], axis=0)
            high, low = split(both)
            right = jnp.concatenate([high, low], axis=0).T
            full = dot(w_high, right)
            full = (
                full[:, : LANES // 2] + full[:, LANES // 2 :] + dot(w_low, right[:, : LANES // 2])
            )
            full = full.reshape(kz_count, channels, LANES // 2)
            result = jnp.zeros((channels, LANES // 2), F32)
            for kz in range(kz_count):
                result = jnp.where(lane == kz, full[kz], result)
            dmodes_ref[j, plane] = jnp.concatenate(
                [result[: channels // 2], result[channels // 2 :]], axis=1
            )
        return 0

    lax.fori_loop(0, owned, body, 0)


def weight_grad_kernel(modes_ref, dmixed_ref, grad_ref):
    owned, planes = modes_ref.shape[:2]
    kz_count, channels = grad_ref.shape[1:3]
    assert planes * channels == LANES
    half = channels // 2
    low_lane = lax.broadcasted_iota(jnp.int32, (half, LANES), 1) < channels
    lane = lax.broadcasted_iota(jnp.int32, (2 * channels, LANES), 1) & (kz_count - 1)

    def body(j, _):
        right = []
        for plane in range(planes):
            rows = transpose_in(dmixed_ref[j, plane])
            right += [rows, turn_down(rows)]
        right = jnp.concatenate(split(jnp.concatenate(right, axis=0)), axis=1)
        first, second = modes_ref[j, 0], modes_ref[j, 1]
        left = jnp.concatenate(
            [
                jnp.where(low_lane, first, pltpu.roll(second, channels, 1)),
                jnp.where(low_lane, pltpu.roll(first, channels, 1), second),
            ],
            axis=0,
        )
        left = jnp.concatenate(split(left), axis=0)
        for kz in range(kz_count):
            full = dot(jnp.where(lane == kz, left, jnp.zeros_like(left)), right)
            grad_ref[j, kz] = (
                full[:channels, :LANES] + full[:channels, LANES:] + full[channels:, :LANES]
            )
        return 0

    lax.fori_loop(0, owned, body, 0)


def input_grad_kernel(
    local_ref, front_ref, back_ref, synth_ref, back_table_ref, out_ref, out_scr, lhs_ref, sems
):
    cells, planes, channels, span = local_ref.shape
    copies = []
    for i, (p, at) in enumerate(chunks(cells, planes)):
        if at == 0:
            from_modes(front_ref, back_ref, back_table_ref, lhs_ref.at[p], p)
        rows = pl.ds(at, STEP)
        spectral = synthesise(lhs_ref.at[p], at, STEP, synth_ref)
        out_scr[i] = spectral.reshape(STEP, channels, span) + local_ref[rows, p]
        copies.append(pltpu.make_async_copy(out_scr.at[i], out_ref.at[rows, p], sems.at[i]))
        copies[-1].start()
    for copy in copies:
        copy.wait()


def swap(values, mask):
    count = lax.axis_size("stream")
    return lax.ppermute(values, "stream", [(i, i ^ mask) for i in range(count)])


def beside(moved, work):
    return lax.optimization_barrier((moved, work()))


def scatter_sum(keep, send, work):
    pieces = [keep, swap(send, 1)]

    def part(first, count):
        total = pieces[0][first : first + count]
        for piece in pieces[1:]:
            total = total + piece[first : first + count]
        return total

    quarter = keep.shape[0] // 4
    moved = [swap(part(quarter * place, quarter), 2 * place) for place in (2, 3, 1)]
    moved, done = beside(moved, work)
    pieces += moved
    for mask in stage_masks()[3:]:
        quarter //= 2
        pieces.append(swap(part(quarter, quarter), mask))
    return pieces, done


def gather_all(values, work=None):
    for mask in reversed(stage_masks()[3:]):
        values = jnp.concatenate([values, swap(values, mask)], axis=0)
    moved = [swap(values, 2 * place) for place in (3, 2, 1)]
    done = None
    if work is not None:
        moved, done = beside(moved, work)
    values = jnp.concatenate([values] + moved[::-1], axis=0)
    return values, swap(values, 1), done


def params():
    return pltpu.CompilerParams(vmem_limit_bytes=VMEM_LIMIT)


def whole(array):
    rank = len(array.shape)
    return pl.BlockSpec(array.shape, lambda *_: (0,) * rank)


def per_device(snapshot, mode_weight, local_weight, offset_bias, upstream):
    cells, planes, span, channels = snapshot.shape
    owned, kz_count = mode_weight.shape[:2]
    total_modes = owned * lax.axis_size("stream")
    half_modes = total_modes // 2
    half_channels = channels // 2
    shape = jax.ShapeDtypeStruct
    x = jnp.swapaxes(snapshot, 2, 3)
    up = jnp.swapaxes(upstream, 2, 3)
    scale = float(cells * lax.axis_size("stream") * span)
    ana_fwd, ana_inv, syn_fwd, syn_inv = map(jnp.asarray, span_tables(span, kz_count, scale))
    pieces_of = len(chunks(cells, planes))
    coef_scr = pltpu.VMEM((planes, half_channels // SUB, 2 * cells * SUB, LANES), F32)
    lhs_scr = pltpu.VMEM((planes, cells, channels, LANES), F32)
    span_scr = pltpu.VMEM((pieces_of, STEP, channels, span), F32)
    sem_scr = pltpu.SemaphoreType.DMA((pieces_of + 1,))
    down = shape((2, total_modes * SUB, 2 * cells * SUB), BF16)
    back = shape((2, 2 * cells * SUB, total_modes * SUB), BF16)
    here = pl.BlockSpec(memory_space=pltpu.VMEM)
    apart = pl.BlockSpec(memory_space=pl.ANY)
    own_shape = shape((owned, planes, half_channels, LANES), F32)
    half_shape = shape((half_modes, planes, half_channels, LANES), F32)
    grid_shape = shape(x.shape, F32)

    keep, send, down, back = pl.pallas_call(
        functools.partial(spanwise_kernel, (owned, total_modes, cells)),
        in_specs=[apart, apart],
        out_specs=[here] * 4,
        out_shape=[half_shape, half_shape, down, back],
        scratch_shapes=[pltpu.VMEM(ana_fwd.shape, BF16), span_scr, coef_scr, sem_scr],
        compiler_params=params(),
        name="spanwise",
    )(pltpu.with_memory_space_constraint(x, pltpu.HBM), pltpu.with_memory_space_constraint(ana_fwd, pltpu.HBM))

    def local_forward():
        return pl.pallas_call(
            functools.partial(pointwise_kernel, True),
            in_specs=[here] * 3,
            out_specs=here,
            out_shape=grid_shape,
            compiler_params=params(),
            name="local_forward",
        )(x, local_weight, offset_bias[None])

    pieces, local = scatter_sum(keep, send, local_forward)
    modes, mixed = pl.pallas_call(
        mix_kernel,
        in_specs=[here] * (len(pieces) + 1),
        out_specs=[here] * 2,
        out_shape=[own_shape] * 2,
        compiler_params=params(),
        name="mix",
    )(*pieces, mode_weight)
    front, behind, _ = gather_all(mixed)
    act, dpre, keep, send = pl.pallas_call(
        middle_kernel,
        in_specs=[here] * 8,
        out_specs=[here] * 4,
        out_shape=[grid_shape, grid_shape, half_shape, half_shape],
        scratch_shapes=[lhs_scr, coef_scr],
        compiler_params=params(),
        name="middle",
    )(local, up, front, behind, syn_inv, ana_inv, down, back)

    def local_backward():
        return pl.pallas_call(
            lambda values, weight, out: pointwise_kernel(False, values, weight, None, out),
            in_specs=[here] * 2,
            out_specs=here,
            out_shape=grid_shape,
            compiler_params=params(),
            name="local_backward",
        )(dpre, local_weight)

    pieces, local = scatter_sum(keep, send, local_backward)
    dmixed, dmodes = pl.pallas_call(
        adjoint_kernel,
        in_specs=[here] * (len(pieces) + 1),
        out_specs=[here] * 2,
        out_shape=[own_shape] * 2,
        compiler_params=params(),
        name="adjoint",
    )(*pieces, mode_weight)

    def weight_grad():
        return pl.pallas_call(
            weight_grad_kernel,
            in_specs=[here] * 2,
            out_specs=here,
            out_shape=shape(mode_weight.shape, F32),
            compiler_params=params(),
            name="weight_grad",
        )(modes, dmixed)

    front, behind, grad_modes = gather_all(dmodes, weight_grad)
    grad_snapshot = pl.pallas_call(
        input_grad_kernel,
        in_specs=[here] * 5,
        out_specs=apart,
        out_shape=grid_shape,
        scratch_shapes=[span_scr, lhs_scr, sem_scr],
        compiler_params=params(),
        name="input_grad",
    )(local, front, behind, syn_fwd, back)
    return jnp.swapaxes(act, 2, 3), jnp.swapaxes(grad_snapshot, 2, 3), grad_modes


def solution(mesh):
    wide = P("stream", "group", None, None)
    return jax.shard_map(
        per_device,
        mesh=mesh,
        in_specs=(wide, P("stream", None, None, None), P(), P(), wide),
        out_specs=(wide, wide, wide),
        check_vma=False,
    )
```

```python
import functools
import math

import jax
import jax.numpy as jnp
import numpy as np
from jax import lax
from jax.experimental import pallas as pl
from jax.experimental.pallas import tpu as pltpu
from jax.sharding import PartitionSpec as P

F32 = jnp.float32
BF16 = jnp.bfloat16
LANES = 128
SUB = 8
VMEM_LIMIT = 16 << 20
STEP = 8
PART = 2


def split_np(values):
    values = values.astype(np.float32)
    high = values.astype(BF16)
    low = (values - high.astype(np.float32)).astype(BF16)
    return high, low


def span_tables(length, modes, scale):
    angle = 2.0 * np.pi * (np.outer(np.arange(length), np.arange(modes)) % length) / length
    forward = np.concatenate([np.cos(angle), -np.sin(angle)], axis=1)
    factor = np.where(np.arange(modes) == 0, 1.0, 2.0) / scale
    backward = forward * np.concatenate([factor, factor])[None, :]

    def analysis(table):
        flipped = np.concatenate([table[:, modes:], -table[:, :modes]], axis=1)
        both = np.concatenate([table, flipped], axis=1)
        return np.concatenate(split_np(both), axis=1)

    def synthesis(table):
        high, low = split_np(table.T)
        return np.concatenate([high, low, high, np.zeros_like(high)], axis=0)

    return analysis(forward), analysis(backward), synthesis(forward), synthesis(backward)


def stage_masks():
    count = lax.axis_size("stream")
    bits = count.bit_length() - 1
    assert 1 << bits == count and bits >= 3
    return [1, 4, 2] + [1 << i for i in range(3, bits)]


def mode_angles(position, inner, cell, owned, total_modes, cells):
    me = lax.axis_index("stream")
    masks = stage_masks()
    steps = len(masks)
    length = cells * (1 << steps)
    assert length & (length - 1) == 0
    bits = [position >> (steps - 1 - step) & 1 for step in range(steps)]
    block = jnp.zeros_like(position) + me
    for bit, mask in zip(bits, masks):
        block = block ^ bit * mask
    rows = block * owned + inner
    wave = jnp.where(rows < total_modes // 2, rows, rows - total_modes)
    phase = wave * (me * cells + cell) & (length - 1)
    phase = jnp.where(phase > length // 2, phase - length, phase)
    return phase.astype(F32) * (2.0 * math.pi / length)


def split(values):
    high = values.astype(BF16)
    return high, (values - high.astype(F32)).astype(BF16)


def dot(left, right):
    return jnp.dot(left, right, preferred_element_type=F32)


def make_tables(down_ref, back_ref, owned, total_modes, cells):
    def iota(shape, axis):
        return lax.broadcasted_iota(jnp.int32, shape, axis)

    def expand(table, ref):
        rows, lanes = table.shape
        full = jnp.broadcast_to(table[:, None, :], (rows, SUB, lanes)).reshape(rows * SUB, lanes)
        same = (iota(full.shape, 0) & (SUB - 1)) == (iota(full.shape, 1) & (SUB - 1))
        high, low = split(jnp.where(same, full, 0.0))
        ref[0] = high
        ref[1] = low

    def table(shape, mode_axis):
        mode = iota(shape, mode_axis)
        cell = iota(shape, 1 - mode_axis)
        if mode_axis == 1:
            mode = mode >> 3
        else:
            cell = cell >> 3
        shift = owned.bit_length() - 1
        angles = mode_angles(
            mode >> shift, mode & (owned - 1), cell & (cells - 1), owned, total_modes, cells
        )
        return jnp.where(cell < cells, jnp.cos(angles), jnp.sin(angles))

    expand(table((total_modes, 2 * cells * SUB), 0), down_ref)
    expand(table((2 * cells, total_modes * SUB), 1), back_ref)


def analyse(values_high, values_low, table_ref, at, coef_ref):
    full = dot(values_high, table_ref[...])
    full = full[:, :LANES] + full[:, LANES:] + dot(values_low, table_ref[:, :LANES])
    cells = coef_ref.shape[1] // (2 * SUB)
    half = 4 * SUB
    low_lane = lax.broadcasted_iota(jnp.int32, (half, LANES), 1) < LANES // 2
    for i in range(full.shape[0] // (2 * half)):
        low = full[2 * half * i : 2 * half * i + half]
        high = full[2 * half * i + half : 2 * half * (i + 1)]
        plain = jnp.where(low_lane, low, pltpu.roll(high, LANES // 2, 1))
        flipped = jnp.where(low_lane, pltpu.roll(low, LANES // 2, 1), high)
        for block in range(half // SUB):
            rows = slice(SUB * block, SUB * (block + 1))
            coef_ref[block, pl.ds((at + i) * SUB, SUB)] = plain[rows]
            coef_ref[block, pl.ds((cells + at + i) * SUB, SUB)] = flipped[rows]


def to_modes(coef_ref, table_ref, out_ref, upper):
    modes, planes = out_ref.shape[:2]
    count = modes * SUB
    rows = slice(count * upper, count * (upper + 1))
    for plane in range(planes):
        for block in range(coef_ref.shape[1]):
            high, low = split(coef_ref[plane, block])
            full = dot(table_ref[0, rows], jnp.concatenate([high, low], axis=1))
            full = full[:, :LANES] + full[:, LANES:] + dot(table_ref[1, rows], high)
            out_ref[:, plane, SUB * block : SUB * (block + 1)] = full.reshape(modes, SUB, LANES)


def from_modes(modes_ref, table_ref, upper, plane, block):
    count = modes_ref.shape[0] * SUB
    lanes = slice(count * upper, count * (upper + 1))
    half = table_ref.shape[1] // 2
    lane = lax.broadcasted_iota(jnp.int32, (half, LANES), 1)
    real = lane % (LANES // 2) < LANES // 4
    values = modes_ref[:, plane, SUB * block : SUB * (block + 1)]
    high, low = split(values.reshape(count, LANES))
    full = dot(table_ref[0, :, lanes], jnp.concatenate([high, low], axis=1))
    full = full[:, :LANES] + full[:, LANES:] + dot(table_ref[1, :, lanes], high)
    plain, other = full[:half], full[half:]
    turned = jnp.where(
        real, -pltpu.roll(other, 3 * LANES // 4, 1), pltpu.roll(other, LANES // 4, 1)
    )
    return plain + turned


def finish_modes(modes_ref, table_ref, inv_ref, lhs_ref, plane):
    cells, channels = lhs_ref.shape[1:3]
    half = channels // 2
    low_lane = lax.broadcasted_iota(jnp.int32, (cells * SUB, LANES), 1) < LANES // 2
    for block in range(half // SUB):
        inv = inv_ref[plane, block] + from_modes(modes_ref, table_ref, 1, plane, block)
        swapped = pltpu.roll(inv, LANES // 2, 1)
        for at, doubled in (
            (0, jnp.where(low_lane, inv, swapped)),
            (half, jnp.where(low_lane, swapped, inv)),
        ):
            lhs_ref[plane, :, at + SUB * block : at + SUB * (block + 1)] = doubled.reshape(
                cells, SUB, LANES
            )


def synthesise(lhs_ref, first, count, table_ref):
    values = lhs_ref[pl.ds(first, count)]
    high, low = split(values.reshape(-1, LANES))
    return dot(jnp.concatenate([high, low], axis=1), table_ref[...])


TAIL_AT = 1.0 / 0.28
TAIL = tuple(
    math.sqrt(2.0 * math.pi) * factor * TAIL_AT ** (power + 1)
    for power, factor in enumerate(
        (
            0.11650589762013625,
            0.06758867364360233,
            0.2686846227283619,
            -0.23671861048677273,
            0.38970758618179535,
            -0.10576817864886755,
        )
    )
)
BELL = (-0.5 * math.log2(math.e), -0.5 * math.log2(2.0 * math.pi))


def normal_parts(values):
    density = jnp.exp2(values * values * BELL[0] + BELL[1])
    inner = 1.0 / (TAIL_AT + jnp.abs(values))
    tail = TAIL[-1] * inner
    for factor in TAIL[-2::-1]:
        tail = (tail + factor) * inner
    tail = tail * density
    return jnp.where(values >= 0.0, 1.0 - tail, tail), density


def transpose_out(rows):
    parts = []
    for half in range(2):
        for part in range(2):
            shift = part * (LANES // 2) + half * (LANES // 4)
            parts.append(pltpu.roll(rows, LANES - shift, 1) if shift else rows)
    return jnp.concatenate(parts, axis=0).T[: LANES // 4]


def transpose_in(values):
    quarter = LANES // 4
    turned = jnp.concatenate([values] * 4, axis=0).T
    lane = lax.broadcasted_iota(jnp.int32, (quarter, LANES), 1) // quarter
    result = turned[:quarter]
    for half in range(2):
        for part in range(2):
            rows = turned[quarter * (2 * half + part) : quarter * (2 * half + part + 1)]
            result = jnp.where(lane == 2 * part + half, rows, result)
    return result


def turn_down(rows):
    lane = lax.broadcasted_iota(jnp.int32, rows.shape, 1) < LANES // 2
    rolled = pltpu.roll(rows, LANES // 2, 1)
    return jnp.where(lane, rolled, -rolled)


def chunks(cells, planes):
    return [(p, at) for p in range(planes) for at in range(0, cells, STEP)]


def spanwise_kernel(
    sizes, x_ref, table_hbm, send_ref, coef_ref, down_ref, back_ref, table_ref, x_scr, sems
):
    cells, planes, channels, span = x_ref.shape
    work = chunks(cells, planes)
    copies = [pltpu.make_async_copy(table_hbm, table_ref, sems.at[len(work) * STEP // PART])]
    for i, (p, at) in enumerate(work):
        for j in range(0, STEP, PART):
            copies.append(
                pltpu.make_async_copy(
                    x_ref.at[pl.ds(at + j, PART), p],
                    x_scr.at[i, pl.ds(j, PART)],
                    sems.at[(i * STEP + j) // PART],
                )
            )
    for copy in copies:
        copy.start()
    make_tables(down_ref, back_ref, *sizes)
    copies.pop(0).wait()
    for i, (p, at) in enumerate(work):
        for j in range(0, STEP, PART):
            copies.pop(0).wait()
        high, low = split(x_scr[i].reshape(STEP * channels, span))
        analyse(high, low, table_ref, at, coef_ref.at[p])
    to_modes(coef_ref, down_ref, send_ref, 1)


def keep_kernel(coef_ref, down_ref, keep_ref):
    to_modes(coef_ref, down_ref, keep_ref, 0)


def front_kernel(front_ref, back_table_ref, inv_ref):
    for plane in range(inv_ref.shape[0]):
        for block in range(inv_ref.shape[1]):
            inv_ref[plane, block] = from_modes(front_ref, back_table_ref, 0, plane, block)


def pointwise_kernel(transposed, values_ref, local_ref, bias_ref, out_ref):
    weight = local_ref[...]
    channels = weight.shape[0]
    if transposed:
        weight = weight.T
    high, low = split(weight)
    lhs = jnp.concatenate([high, high, low], axis=1)
    if bias_ref is not None:
        row = jnp.broadcast_to(bias_ref[...], (channels, channels))
        column = row.T[:, :1]
    cells, planes = values_ref.shape[:2]

    def body(step, _):
        for p in range(planes):
            for cell in range(2):
                at = 2 * step + cell
                high, low = split(values_ref[at, p])
                full = dot(lhs, jnp.concatenate([high, low, high], axis=0))
                out_ref[at, p] = full if bias_ref is None else full + column
        return 0

    lax.fori_loop(0, cells // 2, body, 0)


def total_of(piece_refs, j, plane):
    total = piece_refs[0][j, plane]
    for ref in piece_refs[1:]:
        total = total + ref[j, plane]
    return total


def mix_kernel(*refs):
    *piece_refs, w_ref, modes_ref, mixed_ref = refs
    owned, planes = modes_ref.shape[:2]
    kz_count, channels = w_ref.shape[1:3]
    wide = SUB * channels
    low_lane = lax.broadcasted_iota(jnp.int32, (kz_count, LANES), 1) < channels
    row = lax.broadcasted_iota(jnp.int32, (kz_count, wide), 0) & (SUB - 1)
    own = lax.broadcasted_iota(jnp.int32, (kz_count, wide), 1) // channels == row

    def body(j, _):
        sides = []
        for plane in range(planes):
            total = total_of(piece_refs, j, plane)
            modes_ref[j, plane] = total
            rows = transpose_in(total)
            rolled = pltpu.roll(rows, channels, 1)
            for doubled in (jnp.where(low_lane, rows, rolled), jnp.where(low_lane, rolled, rows)):
                tiled = jnp.concatenate([doubled] * (wide // LANES), axis=1)
                sides.append(jnp.where(own, tiled, 0.0))
        results = []
        for at in range(0, kz_count, SUB):
            left = jnp.concatenate([side[at : at + SUB] for side in sides], axis=0)
            left = jnp.concatenate(split(left), axis=0)
            right = w_ref[j, at : at + SUB].reshape(wide, LANES)
            full = dot(left, jnp.concatenate(split(right), axis=1))
            count = full.shape[0] // 2
            full = full[:count, :LANES] + full[:count, LANES:] + full[count:, :LANES]
            results.append(full.reshape(planes, 2, SUB, LANES))
        for plane in range(planes):
            first, second = (
                jnp.concatenate([result[plane, part] for result in results], axis=0)
                for part in range(2)
            )
            mixed_ref[j, plane] = transpose_out(first - turn_down(second))
        return 0

    lax.fori_loop(0, owned, body, 0)


def middle_kernel(
    local_ref, up_ref, behind_ref, inv_ref, synth_ref, table_ref, down_ref, back_table_ref,
    act_ref, dpre_ref, send_ref, coef_ref, lhs_ref,
):
    cells, planes, channels, span = up_ref.shape
    for p in range(planes):
        finish_modes(behind_ref, back_table_ref, inv_ref, lhs_ref, p)
    for p, at in chunks(cells, planes):
        rows = pl.ds(at, STEP)
        spectral = synthesise(lhs_ref.at[p], at, STEP, synth_ref)
        pre = spectral.reshape(STEP, channels, span) + local_ref[rows, p]
        cumulative, density = normal_parts(pre)
        act_ref[rows, p] = pre * cumulative
        dpre = up_ref[rows, p] * (cumulative + pre * density)
        dpre_ref[rows, p] = dpre
        high, low = split(dpre.reshape(STEP * channels, span))
        analyse(high, low, table_ref, at, coef_ref.at[p])
    to_modes(coef_ref, down_ref, send_ref, 1)


def adjoint_kernel(*refs):
    *piece_refs, w_ref, dmixed_ref, dmodes_ref = refs
    owned, planes = dmixed_ref.shape[:2]
    kz_count, channels, width = w_ref.shape[1:]
    assert planes * channels == LANES
    half = channels // 2
    lane = lax.broadcasted_iota(jnp.int32, (channels, LANES), 1) & (kz_count - 1)
    low_lane = lax.broadcasted_iota(jnp.int32, (half, LANES), 1) < channels

    def body(j, _):
        w_high, w_low = split(w_ref[j].reshape(kz_count * channels, width))
        sides = []
        for plane in range(planes):
            total = total_of(piece_refs, j, plane)
            dmixed_ref[j, plane] = total
            rows = transpose_in(total)
            sides += [rows, turn_down(rows)]
        right = jnp.concatenate(split(jnp.concatenate(sides, axis=0)), axis=0).T
        full = dot(w_high, right)
        full = full[:, :LANES] + full[:, LANES:] + dot(w_low, right[:, :LANES])
        full = full.reshape(kz_count, channels, LANES)
        result = full[0]
        for kz in range(1, kz_count):
            result = jnp.where(lane == kz, full[kz], result)
        low, high = result[:half], result[half:]
        dmodes_ref[j, 0] = jnp.where(low_lane, low, pltpu.roll(high, channels, 1))
        dmodes_ref[j, 1] = jnp.where(low_lane, pltpu.roll(low, channels, 1), high)
        return 0

    lax.fori_loop(0, owned, body, 0)


def weight_grad_kernel(modes_ref, dmixed_ref, grad_ref):
    owned, planes = modes_ref.shape[:2]
    kz_count, channels = grad_ref.shape[1:3]
    assert planes * channels == LANES
    half = channels // 2
    low_lane = lax.broadcasted_iota(jnp.int32, (half, LANES), 1) < channels
    lane = lax.broadcasted_iota(jnp.int32, (2 * channels, LANES), 1) & (kz_count - 1)

    def body(j, _):
        right = []
        for plane in range(planes):
            rows = transpose_in(dmixed_ref[j, plane])
            right += [rows, turn_down(rows)]
        right = jnp.concatenate(split(jnp.concatenate(right, axis=0)), axis=1)
        first, second = modes_ref[j, 0], modes_ref[j, 1]
        left = jnp.concatenate(
            [
                jnp.where(low_lane, first, pltpu.roll(second, channels, 1)),
                jnp.where(low_lane, pltpu.roll(first, channels, 1), second),
            ],
            axis=0,
        )
        left = jnp.concatenate(split(left), axis=0)
        for kz in range(kz_count):
            full = dot(jnp.where(lane == kz, left, jnp.zeros_like(left)), right)
            grad_ref[j, kz] = (
                full[:channels, :LANES] + full[:channels, LANES:] + full[channels:, :LANES]
            )
        return 0

    lax.fori_loop(0, owned, body, 0)


def input_grad_kernel(
    local_ref, behind_ref, inv_ref, synth_ref, back_table_ref, out_ref, out_scr, lhs_ref, sems
):
    cells, planes, channels, span = local_ref.shape
    copies = []
    for i, (p, at) in enumerate(chunks(cells, planes)):
        if at == 0:
            finish_modes(behind_ref, back_table_ref, inv_ref, lhs_ref, p)
        rows = pl.ds(at, STEP)
        spectral = synthesise(lhs_ref.at[p], at, STEP, synth_ref)
        out_scr[i] = spectral.reshape(STEP, channels, span) + local_ref[rows, p]
        copies.append(pltpu.make_async_copy(out_scr.at[i], out_ref.at[rows, p], sems.at[i]))
        copies[-1].start()
    for copy in copies:
        copy.wait()


def swap(values, mask):
    count = lax.axis_size("stream")
    return lax.ppermute(values, "stream", [(i, i ^ mask) for i in range(count)])


def beside(moved, work):
    return lax.optimization_barrier((moved, work()))


def scatter_sum(send, keep_work, work):
    moved, keep = beside(swap(send, 1), keep_work)
    pieces = [keep, moved]

    def part(first, count):
        total = pieces[0][first : first + count]
        for piece in pieces[1:]:
            total = total + piece[first : first + count]
        return total

    quarter = keep.shape[0] // 4
    moved = [swap(part(quarter * place, quarter), 2 * place) for place in (3, 2, 1)]
    moved, done = beside(moved, work)
    pieces += moved
    for mask in stage_masks()[3:]:
        quarter //= 2
        pieces.append(swap(part(quarter, quarter), mask))
    return pieces, done


def gather_all(values, front_work, work=None):
    for mask in reversed(stage_masks()[3:]):
        values = jnp.concatenate([values, swap(values, mask)], axis=0)
    moved = {place: swap(values, 2 * place) for place in (3, 1, 2)}
    done = None
    if work is not None:
        moved, done = beside(moved, work)
    values = jnp.concatenate([values, moved[1], moved[2], moved[3]], axis=0)
    behind, inv = beside(swap(values, 1), lambda: front_work(values))
    return behind, inv, done


def params():
    return pltpu.CompilerParams(vmem_limit_bytes=VMEM_LIMIT)


def whole(array):
    rank = len(array.shape)
    return pl.BlockSpec(array.shape, lambda *_: (0,) * rank)


def per_device(snapshot, mode_weight, local_weight, offset_bias, upstream):
    cells, planes, span, channels = snapshot.shape
    owned, kz_count = mode_weight.shape[:2]
    total_modes = owned * lax.axis_size("stream")
    half_modes = total_modes // 2
    half_channels = channels // 2
    shape = jax.ShapeDtypeStruct
    x = jnp.swapaxes(snapshot, 2, 3)
    up = jnp.swapaxes(upstream, 2, 3)
    scale = float(cells * lax.axis_size("stream") * span)
    ana_fwd, ana_inv, syn_fwd, syn_inv = map(jnp.asarray, span_tables(span, kz_count, scale))
    pieces_of = len(chunks(cells, planes))
    coef_shape = shape((planes, half_channels // SUB, 2 * cells * SUB, LANES), F32)
    inv_shape = shape((planes, half_channels // SUB, cells * SUB, LANES), F32)
    lhs_scr = pltpu.VMEM((planes, cells, channels, LANES), F32)
    span_scr = pltpu.VMEM((pieces_of, STEP, channels, span), F32)
    sem_scr = pltpu.SemaphoreType.DMA((pieces_of * STEP // PART + 1,))
    down = shape((2, total_modes * SUB, 2 * cells * SUB), BF16)
    back = shape((2, 2 * cells * SUB, total_modes * SUB), BF16)
    here = pl.BlockSpec(memory_space=pltpu.VMEM)
    apart = pl.BlockSpec(memory_space=pl.ANY)
    own_shape = shape((owned, planes, half_channels, LANES), F32)
    half_shape = shape((half_modes, planes, half_channels, LANES), F32)
    grid_shape = shape(x.shape, F32)

    send, coef, down, back = pl.pallas_call(
        functools.partial(spanwise_kernel, (owned, total_modes, cells)),
        in_specs=[apart, apart],
        out_specs=[here] * 4,
        out_shape=[half_shape, coef_shape, down, back],
        scratch_shapes=[pltpu.VMEM(ana_fwd.shape, BF16), span_scr, sem_scr],
        compiler_params=params(),
        name="spanwise",
    )(pltpu.with_memory_space_constraint(x, pltpu.HBM), pltpu.with_memory_space_constraint(ana_fwd, pltpu.HBM))

    def keep_part(coef):
        return lambda: pl.pallas_call(
            keep_kernel,
            in_specs=[here] * 2,
            out_specs=here,
            out_shape=half_shape,
            compiler_params=params(),
            name="keep_part",
        )(coef, down)

    def front_part(front):
        return pl.pallas_call(
            front_kernel,
            in_specs=[here] * 2,
            out_specs=here,
            out_shape=inv_shape,
            compiler_params=params(),
            name="front_part",
        )(front, back)

    def local_forward():
        return pl.pallas_call(
            functools.partial(pointwise_kernel, True),
            in_specs=[here] * 3,
            out_specs=here,
            out_shape=grid_shape,
            compiler_params=params(),
            name="local_forward",
        )(x, local_weight, offset_bias[None])

    pieces, local = scatter_sum(send, keep_part(coef), local_forward)
    modes, mixed = pl.pallas_call(
        mix_kernel,
        in_specs=[here] * (len(pieces) + 1),
        out_specs=[here] * 2,
        out_shape=[own_shape] * 2,
        compiler_params=params(),
        name="mix",
    )(*pieces, mode_weight)
    behind, inv, _ = gather_all(mixed, front_part)
    act, dpre, send, coef = pl.pallas_call(
        middle_kernel,
        in_specs=[here] * 8,
        out_specs=[here] * 4,
        out_shape=[grid_shape, grid_shape, half_shape, coef_shape],
        scratch_shapes=[lhs_scr],
        compiler_params=params(),
        name="middle",
    )(local, up, behind, inv, syn_inv, ana_inv, down, back)

    def local_backward():
        return pl.pallas_call(
            lambda values, weight, out: pointwise_kernel(False, values, weight, None, out),
            in_specs=[here] * 2,
            out_specs=here,
            out_shape=grid_shape,
            compiler_params=params(),
            name="local_backward",
        )(dpre, local_weight)

    pieces, local = scatter_sum(send, keep_part(coef), local_backward)
    dmixed, dmodes = pl.pallas_call(
        adjoint_kernel,
        in_specs=[here] * (len(pieces) + 1),
        out_specs=[here] * 2,
        out_shape=[own_shape] * 2,
        compiler_params=params(),
        name="adjoint",
    )(*pieces, mode_weight)

    def weight_grad():
        return pl.pallas_call(
            weight_grad_kernel,
            in_specs=[here] * 2,
            out_specs=here,
            out_shape=shape(mode_weight.shape, F32),
            compiler_params=params(),
            name="weight_grad",
        )(modes, dmixed)

    behind, inv, grad_modes = gather_all(dmodes, front_part, weight_grad)
    grad_snapshot = pl.pallas_call(
        input_grad_kernel,
        in_specs=[here] * 5,
        out_specs=apart,
        out_shape=grid_shape,
        scratch_shapes=[span_scr, lhs_scr, sem_scr],
        compiler_params=params(),
        name="input_grad",
    )(local, behind, inv, syn_fwd, back)
    return jnp.swapaxes(act, 2, 3), jnp.swapaxes(grad_snapshot, 2, 3), grad_modes


def solution(mesh):
    wide = P("stream", "group", None, None)
    return jax.shard_map(
        per_device,
        mesh=mesh,
        in_specs=(wide, P("stream", None, None, None), P(), P(), wide),
        out_specs=(wide, wide, wide),
        check_vma=False,
    )
```

```python
import functools
import math

import jax
import jax.numpy as jnp
import numpy as np
from jax import lax
from jax.experimental import pallas as pl
from jax.experimental.pallas import tpu as pltpu
from jax.sharding import PartitionSpec as P

F32 = jnp.float32
BF16 = jnp.bfloat16
LANES = 128
SUB = 8
VMEM_LIMIT = 16 << 20
STEP = 8
PART = 2


def split_np(values):
    values = values.astype(np.float32)
    high = values.astype(BF16)
    low = (values - high.astype(np.float32)).astype(BF16)
    return high, low


def span_tables(length, modes, scale):
    angle = 2.0 * np.pi * (np.outer(np.arange(length), np.arange(modes)) % length) / length
    forward = np.concatenate([np.cos(angle), -np.sin(angle)], axis=1)
    factor = np.where(np.arange(modes) == 0, 1.0, 2.0) / scale
    backward = forward * np.concatenate([factor, factor])[None, :]

    def analysis(table):
        flipped = np.concatenate([table[:, modes:], -table[:, :modes]], axis=1)
        both = np.concatenate([table, flipped], axis=1)
        return np.concatenate(split_np(both), axis=1)

    def synthesis(table):
        high, low = split_np(table.T)
        return np.concatenate([high, low, high, np.zeros_like(high)], axis=0)

    return analysis(forward), analysis(backward), synthesis(forward), synthesis(backward)


def stage_masks():
    count = lax.axis_size("stream")
    bits = count.bit_length() - 1
    assert 1 << bits == count and bits >= 3
    return [1, 4, 2] + [1 << i for i in range(3, bits)]


def mode_angles(position, inner, cell, owned, total_modes, cells):
    me = lax.axis_index("stream")
    masks = stage_masks()
    steps = len(masks)
    length = cells * (1 << steps)
    assert length & (length - 1) == 0
    bits = [position >> (steps - 1 - step) & 1 for step in range(steps)]
    block = jnp.zeros_like(position) + me
    for bit, mask in zip(bits, masks):
        block = block ^ bit * mask
    rows = block * owned + inner
    wave = jnp.where(rows < total_modes // 2, rows, rows - total_modes)
    phase = wave * (me * cells + cell) & (length - 1)
    phase = jnp.where(phase > length // 2, phase - length, phase)
    return phase.astype(F32) * (2.0 * math.pi / length)


def split(values):
    high = values.astype(BF16)
    return high, (values - high.astype(F32)).astype(BF16)


def dot(left, right):
    return jnp.dot(left, right, preferred_element_type=F32)


def make_tables(down_ref, back_ref, owned, total_modes, cells):
    def iota(shape, axis):
        return lax.broadcasted_iota(jnp.int32, shape, axis)

    def expand(table, ref):
        rows, lanes = table.shape
        full = jnp.broadcast_to(table[:, None, :], (rows, SUB, lanes)).reshape(rows * SUB, lanes)
        same = (iota(full.shape, 0) & (SUB - 1)) == (iota(full.shape, 1) & (SUB - 1))
        high, low = split(jnp.where(same, full, 0.0))
        ref[0] = high
        ref[1] = low

    def table(shape, mode_axis):
        mode = iota(shape, mode_axis)
        cell = iota(shape, 1 - mode_axis)
        if mode_axis == 1:
            mode = mode >> 3
        else:
            cell = cell >> 3
        shift = owned.bit_length() - 1
        angles = mode_angles(
            mode >> shift, mode & (owned - 1), cell & (cells - 1), owned, total_modes, cells
        )
        return jnp.where(cell < cells, jnp.cos(angles), jnp.sin(angles))

    expand(table((total_modes, 2 * cells * SUB), 0), down_ref)
    expand(table((2 * cells, total_modes * SUB), 1), back_ref)


def analyse(values_high, values_low, table_ref, at, coef_ref):
    full = dot(values_high, table_ref[...])
    full = full[:, :LANES] + full[:, LANES:] + dot(values_low, table_ref[:, :LANES])
    cells = coef_ref.shape[1] // (2 * SUB)
    half = 4 * SUB
    low_lane = lax.broadcasted_iota(jnp.int32, (half, LANES), 1) < LANES // 2
    for i in range(full.shape[0] // (2 * half)):
        low = full[2 * half * i : 2 * half * i + half]
        high = full[2 * half * i + half : 2 * half * (i + 1)]
        plain = jnp.where(low_lane, low, pltpu.roll(high, LANES // 2, 1))
        flipped = jnp.where(low_lane, pltpu.roll(low, LANES // 2, 1), high)
        for block in range(half // SUB):
            rows = slice(SUB * block, SUB * (block + 1))
            coef_ref[block, pl.ds((at + i) * SUB, SUB)] = plain[rows]
            coef_ref[block, pl.ds((cells + at + i) * SUB, SUB)] = flipped[rows]


def to_modes(coef_ref, table_ref, out_ref, upper):
    modes, planes = out_ref.shape[:2]
    count = modes * SUB
    rows = slice(count * upper, count * (upper + 1))
    for plane in range(planes):
        for block in range(coef_ref.shape[1]):
            high, low = split(coef_ref[plane, block])
            full = dot(table_ref[0, rows], jnp.concatenate([high, low], axis=1))
            full = full[:, :LANES] + full[:, LANES:] + dot(table_ref[1, rows], high)
            out_ref[:, plane, SUB * block : SUB * (block + 1)] = full.reshape(modes, SUB, LANES)


def from_modes(modes_ref, table_ref, upper, plane, block):
    count = modes_ref.shape[0] * SUB
    lanes = slice(count * upper, count * (upper + 1))
    half = table_ref.shape[1] // 2
    lane = lax.broadcasted_iota(jnp.int32, (half, LANES), 1)
    real = lane % (LANES // 2) < LANES // 4
    values = modes_ref[:, plane, SUB * block : SUB * (block + 1)]
    high, low = split(values.reshape(count, LANES))
    full = dot(table_ref[0, :, lanes], jnp.concatenate([high, low], axis=1))
    full = full[:, :LANES] + full[:, LANES:] + dot(table_ref[1, :, lanes], high)
    plain, other = full[:half], full[half:]
    turned = jnp.where(
        real, -pltpu.roll(other, 3 * LANES // 4, 1), pltpu.roll(other, LANES // 4, 1)
    )
    return plain + turned


def finish_modes(modes_ref, table_ref, inv_ref, lhs_ref, plane):
    cells, channels = lhs_ref.shape[1:3]
    half = channels // 2
    low_lane = lax.broadcasted_iota(jnp.int32, (cells * SUB, LANES), 1) < LANES // 2
    for block in range(half // SUB):
        inv = inv_ref[plane, block] + from_modes(modes_ref, table_ref, 1, plane, block)
        swapped = pltpu.roll(inv, LANES // 2, 1)
        for at, doubled in (
            (0, jnp.where(low_lane, inv, swapped)),
            (half, jnp.where(low_lane, swapped, inv)),
        ):
            lhs_ref[plane, :, at + SUB * block : at + SUB * (block + 1)] = doubled.reshape(
                cells, SUB, LANES
            )


def synthesise(lhs_ref, first, count, table_ref):
    values = lhs_ref[pl.ds(first, count)]
    high, low = split(values.reshape(-1, LANES))
    return dot(jnp.concatenate([high, low], axis=1), table_ref[...])


TAIL_AT = 1.0 / 0.28
TAIL = tuple(
    math.sqrt(2.0 * math.pi) * factor * TAIL_AT ** (power + 1)
    for power, factor in enumerate(
        (
            0.11650589762013625,
            0.06758867364360233,
            0.2686846227283619,
            -0.23671861048677273,
            0.38970758618179535,
            -0.10576817864886755,
        )
    )
)
BELL = (-0.5 * math.log2(math.e), -0.5 * math.log2(2.0 * math.pi))


def normal_parts(values):
    density = jnp.exp2(values * values * BELL[0] + BELL[1])
    inner = 1.0 / (TAIL_AT + jnp.abs(values))
    tail = TAIL[-1] * inner
    for factor in TAIL[-2::-1]:
        tail = (tail + factor) * inner
    tail = tail * density
    return jnp.where(values >= 0.0, 1.0 - tail, tail), density


def transpose_out(rows):
    parts = []
    for half in range(2):
        for part in range(2):
            shift = part * (LANES // 2) + half * (LANES // 4)
            parts.append(pltpu.roll(rows, LANES - shift, 1) if shift else rows)
    return jnp.concatenate(parts, axis=0).T[: LANES // 4]


def transpose_in(values):
    quarter = LANES // 4
    turned = jnp.concatenate([values] * 4, axis=0).T
    lane = lax.broadcasted_iota(jnp.int32, (quarter, LANES), 1) // quarter
    result = turned[:quarter]
    for half in range(2):
        for part in range(2):
            rows = turned[quarter * (2 * half + part) : quarter * (2 * half + part + 1)]
            result = jnp.where(lane == 2 * part + half, rows, result)
    return result


def turn_down(rows):
    lane = lax.broadcasted_iota(jnp.int32, rows.shape, 1) < LANES // 2
    rolled = pltpu.roll(rows, LANES // 2, 1)
    return jnp.where(lane, rolled, -rolled)


def chunks(cells, planes):
    return [(p, at) for p in range(planes) for at in range(0, cells, STEP)]


def spanwise_kernel(
    sizes, x_ref, table_hbm, send_ref, coef_ref, down_ref, back_ref, table_ref, x_scr, sems
):
    cells, planes, channels, span = x_ref.shape
    work = chunks(cells, planes)
    copies = [pltpu.make_async_copy(table_hbm, table_ref, sems.at[len(work) * STEP // PART])]
    for i, (p, at) in enumerate(work):
        for j in range(0, STEP, PART):
            copies.append(
                pltpu.make_async_copy(
                    x_ref.at[pl.ds(at + j, PART), p],
                    x_scr.at[i, pl.ds(j, PART)],
                    sems.at[(i * STEP + j) // PART],
                )
            )
    for copy in copies:
        copy.start()
    make_tables(down_ref, back_ref, *sizes)
    copies.pop(0).wait()
    for i, (p, at) in enumerate(work):
        for j in range(0, STEP, PART):
            copies.pop(0).wait()
        high, low = split(x_scr[i].reshape(STEP * channels, span))
        analyse(high, low, table_ref, at, coef_ref.at[p])
    to_modes(coef_ref, down_ref, send_ref, 1)


def keep_kernel(coef_ref, down_ref, keep_ref):
    to_modes(coef_ref, down_ref, keep_ref, 0)


def front_kernel(front_ref, back_table_ref, inv_ref):
    for plane in range(inv_ref.shape[0]):
        for block in range(inv_ref.shape[1]):
            inv_ref[plane, block] = from_modes(front_ref, back_table_ref, 0, plane, block)


def pointwise_kernel(transposed, values_ref, local_ref, bias_ref, out_ref):
    weight = local_ref[...]
    channels = weight.shape[0]
    if transposed:
        weight = weight.T
    high, low = split(weight)
    lhs = jnp.concatenate([high, high, low], axis=1)
    if bias_ref is not None:
        row = jnp.broadcast_to(bias_ref[...], (channels, channels))
        column = row.T[:, :1]
    cells, planes = values_ref.shape[:2]

    def body(step, _):
        for p in range(planes):
            for cell in range(2):
                at = 2 * step + cell
                high, low = split(values_ref[at, p])
                full = dot(lhs, jnp.concatenate([high, low, high], axis=0))
                out_ref[at, p] = full if bias_ref is None else full + column
        return 0

    lax.fori_loop(0, cells // 2, body, 0)


def total_of(piece_refs, j, plane):
    total = piece_refs[0][j, plane]
    for ref in piece_refs[1:]:
        total = total + ref[j, plane]
    return total


def mix_kernel(*refs):
    *piece_refs, w_ref, modes_ref, mixed_ref = refs
    owned, planes = modes_ref.shape[:2]
    kz_count, channels = w_ref.shape[1:3]
    wide = SUB * channels
    low_lane = lax.broadcasted_iota(jnp.int32, (kz_count, LANES), 1) < channels
    row = lax.broadcasted_iota(jnp.int32, (kz_count, wide), 0) & (SUB - 1)
    own = lax.broadcasted_iota(jnp.int32, (kz_count, wide), 1) // channels == row

    def body(j, _):
        sides = []
        for plane in range(planes):
            total = total_of(piece_refs, j, plane)
            modes_ref[j, plane] = total
            rows = transpose_in(total)
            rolled = pltpu.roll(rows, channels, 1)
            for doubled in (jnp.where(low_lane, rows, rolled), jnp.where(low_lane, rolled, rows)):
                tiled = jnp.concatenate([doubled] * (wide // LANES), axis=1)
                sides.append(jnp.where(own, tiled, 0.0))
        results = []
        for at in range(0, kz_count, SUB):
            left = jnp.concatenate([side[at : at + SUB] for side in sides], axis=0)
            left = jnp.concatenate(split(left), axis=0)
            right = w_ref[j, at : at + SUB].reshape(wide, LANES)
            full = dot(left, jnp.concatenate(split(right), axis=1))
            count = full.shape[0] // 2
            full = full[:count, :LANES] + full[:count, LANES:] + full[count:, :LANES]
            results.append(full.reshape(planes, 2, SUB, LANES))
        for plane in range(planes):
            first, second = (
                jnp.concatenate([result[plane, part] for result in results], axis=0)
                for part in range(2)
            )
            mixed_ref[j, plane] = transpose_out(first - turn_down(second))
        return 0

    lax.fori_loop(0, owned, body, 0)


def middle_kernel(
    local_ref, up_ref, behind_ref, inv_ref, synth_ref, table_ref, down_ref, back_table_ref,
    act_ref, dpre_ref, send_ref, coef_ref, lhs_ref,
):
    cells, planes, channels, span = up_ref.shape
    for p in range(planes):
        finish_modes(behind_ref, back_table_ref, inv_ref, lhs_ref, p)
    for p, at in chunks(cells, planes):
        rows = pl.ds(at, STEP)
        spectral = synthesise(lhs_ref.at[p], at, STEP, synth_ref)
        pre = spectral.reshape(STEP, channels, span) + local_ref[rows, p]
        cumulative, density = normal_parts(pre)
        act_ref[rows, p] = pre * cumulative
        dpre = up_ref[rows, p] * (cumulative + pre * density)
        dpre_ref[rows, p] = dpre
        high, low = split(dpre.reshape(STEP * channels, span))
        analyse(high, low, table_ref, at, coef_ref.at[p])
    to_modes(coef_ref, down_ref, send_ref, 1)


def adjoint_kernel(*refs):
    *piece_refs, w_ref, dmixed_ref, dmodes_ref = refs
    owned, planes = dmixed_ref.shape[:2]
    kz_count, channels, width = w_ref.shape[1:]
    assert planes * channels == LANES
    half = channels // 2
    lane = lax.broadcasted_iota(jnp.int32, (channels, LANES), 1) & (kz_count - 1)
    low_lane = lax.broadcasted_iota(jnp.int32, (half, LANES), 1) < channels

    def body(j, _):
        w_high, w_low = split(w_ref[j].reshape(kz_count * channels, width))
        sides = []
        for plane in range(planes):
            total = total_of(piece_refs, j, plane)
            dmixed_ref[j, plane] = total
            rows = transpose_in(total)
            sides += [rows, turn_down(rows)]
        right = jnp.concatenate(split(jnp.concatenate(sides, axis=0)), axis=0).T
        full = dot(w_high, right)
        full = full[:, :LANES] + full[:, LANES:] + dot(w_low, right[:, :LANES])
        full = full.reshape(kz_count, channels, LANES)
        result = full[0]
        for kz in range(1, kz_count):
            result = jnp.where(lane == kz, full[kz], result)
        low, high = result[:half], result[half:]
        dmodes_ref[j, 0] = jnp.where(low_lane, low, pltpu.roll(high, channels, 1))
        dmodes_ref[j, 1] = jnp.where(low_lane, pltpu.roll(low, channels, 1), high)
        return 0

    lax.fori_loop(0, owned, body, 0)


def weight_grad_kernel(modes_ref, dmixed_ref, grad_ref):
    owned, planes = modes_ref.shape[:2]
    kz_count, channels = grad_ref.shape[1:3]
    assert planes * channels == LANES
    half = channels // 2
    low_lane = lax.broadcasted_iota(jnp.int32, (half, LANES), 1) < channels
    lane = lax.broadcasted_iota(jnp.int32, (2 * channels, LANES), 1) & (kz_count - 1)

    def body(j, _):
        right = []
        for plane in range(planes):
            rows = transpose_in(dmixed_ref[j, plane])
            right += [rows, turn_down(rows)]
        right = jnp.concatenate(split(jnp.concatenate(right, axis=0)), axis=1)
        first, second = modes_ref[j, 0], modes_ref[j, 1]
        left = jnp.concatenate(
            [
                jnp.where(low_lane, first, pltpu.roll(second, channels, 1)),
                jnp.where(low_lane, pltpu.roll(first, channels, 1), second),
            ],
            axis=0,
        )
        left = jnp.concatenate(split(left), axis=0)
        for kz in range(kz_count):
            full = dot(jnp.where(lane == kz, left, jnp.zeros_like(left)), right)
            grad_ref[j, kz] = (
                full[:channels, :LANES] + full[:channels, LANES:] + full[channels:, :LANES]
            )
        return 0

    lax.fori_loop(0, owned, body, 0)


def input_grad_kernel(
    local_ref, behind_ref, inv_ref, synth_ref, back_table_ref, out_ref, out_scr, lhs_ref, sems
):
    cells, planes, channels, span = local_ref.shape
    copies = []
    for i, (p, at) in enumerate(chunks(cells, planes)):
        if at == 0:
            finish_modes(behind_ref, back_table_ref, inv_ref, lhs_ref, p)
        rows = pl.ds(at, STEP)
        spectral = synthesise(lhs_ref.at[p], at, STEP, synth_ref)
        out_scr[i] = spectral.reshape(STEP, channels, span) + local_ref[rows, p]
        copies.append(pltpu.make_async_copy(out_scr.at[i], out_ref.at[rows, p], sems.at[i]))
        copies[-1].start()
    for copy in copies:
        copy.wait()


def swap(values, mask):
    count = lax.axis_size("stream")
    return lax.ppermute(values, "stream", [(i, i ^ mask) for i in range(count)])


def beside(moved, work):
    return lax.optimization_barrier((moved, work()))


def scatter_sum(send, keep_work, work):
    moved, keep = beside(swap(send, 1), keep_work)
    pieces = [keep, moved]

    def part(first, count):
        total = pieces[0][first : first + count]
        for piece in pieces[1:]:
            total = total + piece[first : first + count]
        return total

    quarter = keep.shape[0] // 4
    moved = [swap(part(quarter * place, quarter), 2 * place) for place in (3, 1, 2)]
    moved, done = beside(moved, work)
    pieces += moved
    for mask in stage_masks()[3:]:
        quarter //= 2
        pieces.append(swap(part(quarter, quarter), mask))
    return pieces, done


def gather_all(values, front_work, work=None):
    for mask in reversed(stage_masks()[3:]):
        values = jnp.concatenate([values, swap(values, mask)], axis=0)
    order = (1, 3, 2) if work is None else (3, 1, 2)
    moved = {place: swap(values, 2 * place) for place in order}
    done = None
    if work is not None:
        moved, done = beside(moved, work)
    values = jnp.concatenate([values, moved[1], moved[2], moved[3]], axis=0)
    behind, inv = beside(swap(values, 1), lambda: front_work(values))
    return behind, inv, done


def params():
    return pltpu.CompilerParams(vmem_limit_bytes=VMEM_LIMIT)


def whole(array):
    rank = len(array.shape)
    return pl.BlockSpec(array.shape, lambda *_: (0,) * rank)


def per_device(snapshot, mode_weight, local_weight, offset_bias, upstream):
    cells, planes, span, channels = snapshot.shape
    owned, kz_count = mode_weight.shape[:2]
    total_modes = owned * lax.axis_size("stream")
    half_modes = total_modes // 2
    half_channels = channels // 2
    shape = jax.ShapeDtypeStruct
    x = jnp.swapaxes(snapshot, 2, 3)
    up = jnp.swapaxes(upstream, 2, 3)
    scale = float(cells * lax.axis_size("stream") * span)
    ana_fwd, ana_inv, syn_fwd, syn_inv = map(jnp.asarray, span_tables(span, kz_count, scale))
    pieces_of = len(chunks(cells, planes))
    coef_shape = shape((planes, half_channels // SUB, 2 * cells * SUB, LANES), F32)
    inv_shape = shape((planes, half_channels // SUB, cells * SUB, LANES), F32)
    lhs_scr = pltpu.VMEM((planes, cells, channels, LANES), F32)
    span_scr = pltpu.VMEM((pieces_of, STEP, channels, span), F32)
    sem_scr = pltpu.SemaphoreType.DMA((pieces_of * STEP // PART + 1,))
    down = shape((2, total_modes * SUB, 2 * cells * SUB), BF16)
    back = shape((2, 2 * cells * SUB, total_modes * SUB), BF16)
    here = pl.BlockSpec(memory_space=pltpu.VMEM)
    apart = pl.BlockSpec(memory_space=pl.ANY)
    own_shape = shape((owned, planes, half_channels, LANES), F32)
    half_shape = shape((half_modes, planes, half_channels, LANES), F32)
    grid_shape = shape(x.shape, F32)

    send, coef, down, back = pl.pallas_call(
        functools.partial(spanwise_kernel, (owned, total_modes, cells)),
        in_specs=[apart, apart],
        out_specs=[here] * 4,
        out_shape=[half_shape, coef_shape, down, back],
        scratch_shapes=[pltpu.VMEM(ana_fwd.shape, BF16), span_scr, sem_scr],
        compiler_params=params(),
        name="spanwise",
    )(pltpu.with_memory_space_constraint(x, pltpu.HBM), pltpu.with_memory_space_constraint(ana_fwd, pltpu.HBM))

    def keep_part(coef):
        return lambda: pl.pallas_call(
            keep_kernel,
            in_specs=[here] * 2,
            out_specs=here,
            out_shape=half_shape,
            compiler_params=params(),
            name="keep_part",
        )(coef, down)

    def front_part(front):
        return pl.pallas_call(
            front_kernel,
            in_specs=[here] * 2,
            out_specs=here,
            out_shape=inv_shape,
            compiler_params=params(),
            name="front_part",
        )(front, back)

    def local_forward():
        return pl.pallas_call(
            functools.partial(pointwise_kernel, True),
            in_specs=[here] * 3,
            out_specs=here,
            out_shape=grid_shape,
            compiler_params=params(),
            name="local_forward",
        )(x, local_weight, offset_bias[None])

    pieces, local = scatter_sum(send, keep_part(coef), local_forward)
    modes, mixed = pl.pallas_call(
        mix_kernel,
        in_specs=[here] * (len(pieces) + 1),
        out_specs=[here] * 2,
        out_shape=[own_shape] * 2,
        compiler_params=params(),
        name="mix",
    )(*pieces, mode_weight)
    behind, inv, _ = gather_all(mixed, front_part)
    act, dpre, send, coef = pl.pallas_call(
        middle_kernel,
        in_specs=[here] * 8,
        out_specs=[here] * 4,
        out_shape=[grid_shape, grid_shape, half_shape, coef_shape],
        scratch_shapes=[lhs_scr],
        compiler_params=params(),
        name="middle",
    )(local, up, behind, inv, syn_inv, ana_inv, down, back)

    def local_backward():
        return pl.pallas_call(
            lambda values, weight, out: pointwise_kernel(False, values, weight, None, out),
            in_specs=[here] * 2,
            out_specs=here,
            out_shape=grid_shape,
            compiler_params=params(),
            name="local_backward",
        )(dpre, local_weight)

    pieces, local = scatter_sum(send, keep_part(coef), local_backward)
    dmixed, dmodes = pl.pallas_call(
        adjoint_kernel,
        in_specs=[here] * (len(pieces) + 1),
        out_specs=[here] * 2,
        out_shape=[own_shape] * 2,
        compiler_params=params(),
        name="adjoint",
    )(*pieces, mode_weight)

    def weight_grad():
        return pl.pallas_call(
            weight_grad_kernel,
            in_specs=[here] * 2,
            out_specs=here,
            out_shape=shape(mode_weight.shape, F32),
            compiler_params=params(),
            name="weight_grad",
        )(modes, dmixed)

    behind, inv, grad_modes = gather_all(dmodes, front_part, weight_grad)
    grad_snapshot = pl.pallas_call(
        input_grad_kernel,
        in_specs=[here] * 5,
        out_specs=apart,
        out_shape=grid_shape,
        scratch_shapes=[span_scr, lhs_scr, sem_scr],
        compiler_params=params(),
        name="input_grad",
    )(local, behind, inv, syn_fwd, back)
    return jnp.swapaxes(act, 2, 3), jnp.swapaxes(grad_snapshot, 2, 3), grad_modes


def solution(mesh):
    wide = P("stream", "group", None, None)
    return jax.shard_map(
        per_device,
        mesh=mesh,
        in_specs=(wide, P("stream", None, None, None), P(), P(), wide),
        out_specs=(wide, wide, wide),
        check_vma=False,
    )
```

```python
import functools
import math

import jax
import jax.numpy as jnp
import numpy as np
from jax import lax
from jax.experimental import pallas as pl
from jax.experimental.pallas import tpu as pltpu
from jax.sharding import PartitionSpec as P

F32 = jnp.float32
BF16 = jnp.bfloat16
LANES = 128
SUB = 8
VMEM_LIMIT = 16 << 20
STEP = 8
PART = 2


def split_np(values):
    values = values.astype(np.float32)
    high = values.astype(BF16)
    low = (values - high.astype(np.float32)).astype(BF16)
    return high, low


def span_tables(length, modes, scale):
    angle = 2.0 * np.pi * (np.outer(np.arange(length), np.arange(modes)) % length) / length
    forward = np.concatenate([np.cos(angle), -np.sin(angle)], axis=1)
    factor = np.where(np.arange(modes) == 0, 1.0, 2.0) / scale
    backward = forward * np.concatenate([factor, factor])[None, :]

    def analysis(table):
        flipped = np.concatenate([table[:, modes:], -table[:, :modes]], axis=1)
        both = np.concatenate([table, flipped], axis=1)
        return np.concatenate(split_np(both), axis=1)

    def synthesis(table):
        high, low = split_np(table.T)
        return np.concatenate([high, low, high, np.zeros_like(high)], axis=0)

    return analysis(forward), analysis(backward), synthesis(forward), synthesis(backward)


def stage_masks():
    count = lax.axis_size("stream")
    bits = count.bit_length() - 1
    assert 1 << bits == count and bits >= 3
    return [1, 4, 2] + [1 << i for i in range(3, bits)]


def mode_angles(position, inner, cell, owned, total_modes, cells):
    me = lax.axis_index("stream")
    masks = stage_masks()
    steps = len(masks)
    length = cells * (1 << steps)
    assert length & (length - 1) == 0
    bits = [position >> (steps - 1 - step) & 1 for step in range(steps)]
    block = jnp.zeros_like(position) + me
    for bit, mask in zip(bits, masks):
        block = block ^ bit * mask
    rows = block * owned + inner
    wave = jnp.where(rows < total_modes // 2, rows, rows - total_modes)
    phase = wave * (me * cells + cell) & (length - 1)
    phase = jnp.where(phase > length // 2, phase - length, phase)
    return phase.astype(F32) * (2.0 * math.pi / length)


def split(values):
    high = values.astype(BF16)
    return high, (values - high.astype(F32)).astype(BF16)


def dot(left, right):
    return jnp.dot(left, right, preferred_element_type=F32)


def make_tables(down_ref, back_ref, owned, total_modes, cells):
    def iota(shape, axis):
        return lax.broadcasted_iota(jnp.int32, shape, axis)

    def expand(table, ref):
        rows, lanes = table.shape
        full = jnp.broadcast_to(table[:, None, :], (rows, SUB, lanes)).reshape(rows * SUB, lanes)
        same = (iota(full.shape, 0) & (SUB - 1)) == (iota(full.shape, 1) & (SUB - 1))
        high, low = split(jnp.where(same, full, 0.0))
        ref[0] = high
        ref[1] = low

    def table(shape, mode_axis):
        mode = iota(shape, mode_axis)
        cell = iota(shape, 1 - mode_axis)
        if mode_axis == 1:
            mode = mode >> 3
        else:
            cell = cell >> 3
        shift = owned.bit_length() - 1
        angles = mode_angles(
            mode >> shift, mode & (owned - 1), cell & (cells - 1), owned, total_modes, cells
        )
        return jnp.where(cell < cells, jnp.cos(angles), jnp.sin(angles))

    expand(table((total_modes, 2 * cells * SUB), 0), down_ref)
    expand(table((2 * cells, total_modes * SUB), 1), back_ref)


def analyse(values_high, values_low, table_ref, at, coef_ref):
    full = dot(values_high, table_ref[...])
    full = full[:, :LANES] + full[:, LANES:] + dot(values_low, table_ref[:, :LANES])
    cells = coef_ref.shape[1] // (2 * SUB)
    half = 4 * SUB
    low_lane = lax.broadcasted_iota(jnp.int32, (half, LANES), 1) < LANES // 2
    for i in range(full.shape[0] // (2 * half)):
        low = full[2 * half * i : 2 * half * i + half]
        high = full[2 * half * i + half : 2 * half * (i + 1)]
        plain = jnp.where(low_lane, low, pltpu.roll(high, LANES // 2, 1))
        flipped = jnp.where(low_lane, pltpu.roll(low, LANES // 2, 1), high)
        for block in range(half // SUB):
            rows = slice(SUB * block, SUB * (block + 1))
            coef_ref[block, pl.ds((at + i) * SUB, SUB)] = plain[rows]
            coef_ref[block, pl.ds((cells + at + i) * SUB, SUB)] = flipped[rows]


def to_modes(coef_ref, table_ref, out_ref, upper):
    modes, planes = out_ref.shape[:2]
    count = modes * SUB
    rows = slice(count * upper, count * (upper + 1))
    for plane in range(planes):
        for block in range(coef_ref.shape[1]):
            high, low = split(coef_ref[plane, block])
            full = dot(table_ref[0, rows], jnp.concatenate([high, low], axis=1))
            full = full[:, :LANES] + full[:, LANES:] + dot(table_ref[1, rows], high)
            out_ref[:, plane, SUB * block : SUB * (block + 1)] = full.reshape(modes, SUB, LANES)


def from_modes(modes_ref, table_ref, upper, plane, block):
    count = modes_ref.shape[0] * SUB
    lanes = slice(count * upper, count * (upper + 1))
    half = table_ref.shape[1] // 2
    lane = lax.broadcasted_iota(jnp.int32, (half, LANES), 1)
    real = lane % (LANES // 2) < LANES // 4
    values = modes_ref[:, plane, SUB * block : SUB * (block + 1)]
    high, low = split(values.reshape(count, LANES))
    full = dot(table_ref[0, :, lanes], jnp.concatenate([high, low], axis=1))
    full = full[:, :LANES] + full[:, LANES:] + dot(table_ref[1, :, lanes], high)
    plain, other = full[:half], full[half:]
    turned = jnp.where(
        real, -pltpu.roll(other, 3 * LANES // 4, 1), pltpu.roll(other, LANES // 4, 1)
    )
    return plain + turned


def finish_modes(modes_ref, table_ref, inv_ref, lhs_ref, plane):
    cells, channels = lhs_ref.shape[1:3]
    half = channels // 2
    low_lane = lax.broadcasted_iota(jnp.int32, (cells * SUB, LANES), 1) < LANES // 2
    for block in range(half // SUB):
        inv = inv_ref[plane, block] + from_modes(modes_ref, table_ref, 1, plane, block)
        swapped = pltpu.roll(inv, LANES // 2, 1)
        for at, doubled in (
            (0, jnp.where(low_lane, inv, swapped)),
            (half, jnp.where(low_lane, swapped, inv)),
        ):
            lhs_ref[plane, :, at + SUB * block : at + SUB * (block + 1)] = doubled.reshape(
                cells, SUB, LANES
            )


def synthesise(lhs_ref, first, count, table_ref):
    values = lhs_ref[pl.ds(first, count)]
    high, low = split(values.reshape(-1, LANES))
    return dot(jnp.concatenate([high, low], axis=1), table_ref[...])


TAIL_AT = 1.0 / 0.28
TAIL = tuple(
    math.sqrt(2.0 * math.pi) * factor * TAIL_AT ** (power + 1)
    for power, factor in enumerate(
        (
            0.11650589762013625,
            0.06758867364360233,
            0.2686846227283619,
            -0.23671861048677273,
            0.38970758618179535,
            -0.10576817864886755,
        )
    )
)
BELL = (-0.5 * math.log2(math.e), -0.5 * math.log2(2.0 * math.pi))


def normal_parts(values):
    density = jnp.exp2(values * values * BELL[0] + BELL[1])
    inner = 1.0 / (TAIL_AT + jnp.abs(values))
    tail = TAIL[-1] * inner
    for factor in TAIL[-2::-1]:
        tail = (tail + factor) * inner
    tail = tail * density
    return jnp.where(values >= 0.0, 1.0 - tail, tail), density


def transpose_out(rows):
    parts = []
    for half in range(2):
        for part in range(2):
            shift = part * (LANES // 2) + half * (LANES // 4)
            parts.append(pltpu.roll(rows, LANES - shift, 1) if shift else rows)
    return jnp.concatenate(parts, axis=0).T[: LANES // 4]


def transpose_in(values):
    quarter = LANES // 4
    turned = jnp.concatenate([values] * 4, axis=0).T
    lane = lax.broadcasted_iota(jnp.int32, (quarter, LANES), 1) // quarter
    result = turned[:quarter]
    for half in range(2):
        for part in range(2):
            rows = turned[quarter * (2 * half + part) : quarter * (2 * half + part + 1)]
            result = jnp.where(lane == 2 * part + half, rows, result)
    return result


def turn_down(rows):
    lane = lax.broadcasted_iota(jnp.int32, rows.shape, 1) < LANES // 2
    rolled = pltpu.roll(rows, LANES // 2, 1)
    return jnp.where(lane, rolled, -rolled)


def chunks(cells, planes, step=STEP):
    return [(p, at) for p in range(planes) for at in range(0, cells, step)]


def spanwise_kernel(
    sizes, x_ref, table_hbm, send_ref, coef_ref, down_ref, back_ref, table_ref, x_scr, sems
):
    cells, planes, channels, span = x_ref.shape
    work = chunks(cells, planes)
    copies = [pltpu.make_async_copy(table_hbm, table_ref, sems.at[len(work) * STEP // PART])]
    for i, (p, at) in enumerate(work):
        for j in range(0, STEP, PART):
            copies.append(
                pltpu.make_async_copy(
                    x_ref.at[pl.ds(at + j, PART), p],
                    x_scr.at[i, pl.ds(j, PART)],
                    sems.at[(i * STEP + j) // PART],
                )
            )
    for copy in copies:
        copy.start()
    make_tables(down_ref, back_ref, *sizes)
    copies.pop(0).wait()
    for i, (p, at) in enumerate(work):
        for j in range(0, STEP, PART):
            copies.pop(0).wait()
        high, low = split(x_scr[i].reshape(STEP * channels, span))
        analyse(high, low, table_ref, at, coef_ref.at[p])
    to_modes(coef_ref, down_ref, send_ref, 1)


def keep_kernel(coef_ref, down_ref, keep_ref):
    to_modes(coef_ref, down_ref, keep_ref, 0)


def front_kernel(front_ref, back_table_ref, inv_ref):
    for plane in range(inv_ref.shape[0]):
        for block in range(inv_ref.shape[1]):
            inv_ref[plane, block] = from_modes(front_ref, back_table_ref, 0, plane, block)


def pointwise_kernel(transposed, values_ref, local_ref, bias_ref, out_ref):
    weight = local_ref[...]
    channels = weight.shape[0]
    if transposed:
        weight = weight.T
    high, low = split(weight)
    lhs = jnp.concatenate([high, high, low], axis=1)
    if bias_ref is not None:
        row = jnp.broadcast_to(bias_ref[...], (channels, channels))
        column = row.T[:, :1]
    cells, planes = values_ref.shape[:2]

    def body(step, _):
        for p in range(planes):
            for cell in range(2):
                at = 2 * step + cell
                high, low = split(values_ref[at, p])
                full = dot(lhs, jnp.concatenate([high, low, high], axis=0))
                out_ref[at, p] = full if bias_ref is None else full + column
        return 0

    lax.fori_loop(0, cells // 2, body, 0)


def total_of(piece_refs, j, plane):
    total = piece_refs[0][j, plane]
    for ref in piece_refs[1:]:
        total = total + ref[j, plane]
    return total


def mix_kernel(*refs):
    *piece_refs, w_ref, modes_ref, mixed_ref = refs
    owned, planes = modes_ref.shape[:2]
    kz_count, channels = w_ref.shape[1:3]
    wide = SUB * channels
    low_lane = lax.broadcasted_iota(jnp.int32, (kz_count, LANES), 1) < channels
    row = lax.broadcasted_iota(jnp.int32, (kz_count, wide), 0) & (SUB - 1)
    own = lax.broadcasted_iota(jnp.int32, (kz_count, wide), 1) // channels == row

    def body(j, _):
        sides = []
        for plane in range(planes):
            total = total_of(piece_refs, j, plane)
            modes_ref[j, plane] = total
            rows = transpose_in(total)
            rolled = pltpu.roll(rows, channels, 1)
            for doubled in (jnp.where(low_lane, rows, rolled), jnp.where(low_lane, rolled, rows)):
                tiled = jnp.concatenate([doubled] * (wide // LANES), axis=1)
                sides.append(jnp.where(own, tiled, 0.0))
        results = []
        for at in range(0, kz_count, SUB):
            left = jnp.concatenate([side[at : at + SUB] for side in sides], axis=0)
            left = jnp.concatenate(split(left), axis=0)
            right = w_ref[j, at : at + SUB].reshape(wide, LANES)
            full = dot(left, jnp.concatenate(split(right), axis=1))
            count = full.shape[0] // 2
            full = full[:count, :LANES] + full[:count, LANES:] + full[count:, :LANES]
            results.append(full.reshape(planes, 2, SUB, LANES))
        for plane in range(planes):
            first, second = (
                jnp.concatenate([result[plane, part] for result in results], axis=0)
                for part in range(2)
            )
            mixed_ref[j, plane] = transpose_out(first - turn_down(second))
        return 0

    lax.fori_loop(0, owned, body, 0)


def middle_kernel(
    local_ref, up_ref, behind_ref, inv_ref, synth_ref, table_ref, down_ref, back_table_ref,
    act_ref, dpre_ref, send_ref, coef_ref, lhs_ref,
):
    cells, planes, channels, span = up_ref.shape
    for p in range(planes):
        finish_modes(behind_ref, back_table_ref, inv_ref, lhs_ref, p)
    for p, at in chunks(cells, planes):
        spectral = synthesise(lhs_ref.at[p], at, STEP, synth_ref)
        spectral = spectral.reshape(STEP, channels, span)
        halves = []
        for cell in range(STEP):
            pre = spectral[cell] + local_ref[at + cell, p]
            cumulative, density = normal_parts(pre)
            act_ref[at + cell, p] = pre * cumulative
            dpre = up_ref[at + cell, p] * (cumulative + pre * density)
            dpre_ref[at + cell, p] = dpre
            halves.append(split(dpre))
        high = jnp.concatenate([half[0] for half in halves], axis=0)
        low = jnp.concatenate([half[1] for half in halves], axis=0)
        analyse(high, low, table_ref, at, coef_ref.at[p])
    to_modes(coef_ref, down_ref, send_ref, 1)


def adjoint_kernel(*refs):
    *piece_refs, w_ref, dmixed_ref, dmodes_ref = refs
    owned, planes = dmixed_ref.shape[:2]
    kz_count, channels, width = w_ref.shape[1:]
    assert planes * channels == LANES
    half = channels // 2
    lane = lax.broadcasted_iota(jnp.int32, (channels, LANES), 1) & (kz_count - 1)
    low_lane = lax.broadcasted_iota(jnp.int32, (half, LANES), 1) < channels

    def body(j, _):
        w_high, w_low = split(w_ref[j].reshape(kz_count * channels, width))
        sides = []
        for plane in range(planes):
            total = total_of(piece_refs, j, plane)
            dmixed_ref[j, plane] = total
            rows = transpose_in(total)
            sides += [rows, turn_down(rows)]
        right = jnp.concatenate(split(jnp.concatenate(sides, axis=0)), axis=0).T
        full = dot(w_high, right)
        full = full[:, :LANES] + full[:, LANES:] + dot(w_low, right[:, :LANES])
        full = full.reshape(kz_count, channels, LANES)
        result = full[0]
        for kz in range(1, kz_count):
            result = jnp.where(lane == kz, full[kz], result)
        low, high = result[:half], result[half:]
        dmodes_ref[j, 0] = jnp.where(low_lane, low, pltpu.roll(high, channels, 1))
        dmodes_ref[j, 1] = jnp.where(low_lane, pltpu.roll(low, channels, 1), high)
        return 0

    lax.fori_loop(0, owned, body, 0)


def weight_grad_kernel(modes_ref, dmixed_ref, grad_ref):
    owned, planes = modes_ref.shape[:2]
    kz_count, channels = grad_ref.shape[1:3]
    assert planes * channels == LANES
    half = channels // 2
    low_lane = lax.broadcasted_iota(jnp.int32, (half, LANES), 1) < channels
    lane = lax.broadcasted_iota(jnp.int32, (2 * channels, LANES), 1) & (kz_count - 1)

    def body(j, _):
        right = []
        for plane in range(planes):
            rows = transpose_in(dmixed_ref[j, plane])
            right += [rows, turn_down(rows)]
        right = jnp.concatenate(split(jnp.concatenate(right, axis=0)), axis=1)
        first, second = modes_ref[j, 0], modes_ref[j, 1]
        left = jnp.concatenate(
            [
                jnp.where(low_lane, first, pltpu.roll(second, channels, 1)),
                jnp.where(low_lane, pltpu.roll(first, channels, 1), second),
            ],
            axis=0,
        )
        left = jnp.concatenate(split(left), axis=0)
        for kz in range(kz_count):
            full = dot(jnp.where(lane == kz, left, jnp.zeros_like(left)), right)
            grad_ref[j, kz] = (
                full[:channels, :LANES] + full[:channels, LANES:] + full[channels:, :LANES]
            )
        return 0

    lax.fori_loop(0, owned, body, 0)


def input_grad_kernel(
    local_ref, behind_ref, inv_ref, synth_ref, back_table_ref, out_ref, out_scr, lhs_ref, sems
):
    cells, planes, channels, span = local_ref.shape
    copies = []
    for i, (p, at) in enumerate(chunks(cells, planes, STEP // 2)):
        if at == 0:
            finish_modes(behind_ref, back_table_ref, inv_ref, lhs_ref, p)
        rows = pl.ds(at, STEP // 2)
        spectral = synthesise(lhs_ref.at[p], at, STEP // 2, synth_ref)
        piece = out_scr.at[i // 2, pl.ds(i % 2 * (STEP // 2), STEP // 2)]
        piece[...] = spectral.reshape(STEP // 2, channels, span) + local_ref[rows, p]
        copies.append(pltpu.make_async_copy(piece, out_ref.at[rows, p], sems.at[i]))
        copies[-1].start()
    for copy in copies:
        copy.wait()


def swap(values, mask):
    count = lax.axis_size("stream")
    return lax.ppermute(values, "stream", [(i, i ^ mask) for i in range(count)])


def beside(moved, work):
    return lax.optimization_barrier((moved, work()))


def scatter_sum(send, keep_work, work):
    moved, keep = beside(swap(send, 1), keep_work)
    pieces = [keep, moved]

    def part(first, count):
        total = pieces[0][first : first + count]
        for piece in pieces[1:]:
            total = total + piece[first : first + count]
        return total

    quarter = keep.shape[0] // 4
    moved = [swap(part(quarter * place, quarter), 2 * place) for place in (3, 1, 2)]
    moved, done = beside(moved, work)
    pieces += moved
    for mask in stage_masks()[3:]:
        quarter //= 2
        pieces.append(swap(part(quarter, quarter), mask))
    return pieces, done


def gather_all(values, front_work, work=None):
    for mask in reversed(stage_masks()[3:]):
        values = jnp.concatenate([values, swap(values, mask)], axis=0)
    order = (1, 3, 2) if work is None else (3, 1, 2)
    moved = {place: swap(values, 2 * place) for place in order}
    done = None
    if work is not None:
        moved, done = beside(moved, work)
    values = jnp.concatenate([values, moved[1], moved[2], moved[3]], axis=0)
    behind, inv = beside(swap(values, 1), lambda: front_work(values))
    return behind, inv, done


def params():
    return pltpu.CompilerParams(vmem_limit_bytes=VMEM_LIMIT)


def whole(array):
    rank = len(array.shape)
    return pl.BlockSpec(array.shape, lambda *_: (0,) * rank)


def per_device(snapshot, mode_weight, local_weight, offset_bias, upstream):
    cells, planes, span, channels = snapshot.shape
    owned, kz_count = mode_weight.shape[:2]
    total_modes = owned * lax.axis_size("stream")
    half_modes = total_modes // 2
    half_channels = channels // 2
    shape = jax.ShapeDtypeStruct
    x = jnp.swapaxes(snapshot, 2, 3)
    up = jnp.swapaxes(upstream, 2, 3)
    scale = float(cells * lax.axis_size("stream") * span)
    ana_fwd, ana_inv, syn_fwd, syn_inv = map(jnp.asarray, span_tables(span, kz_count, scale))
    pieces_of = len(chunks(cells, planes))
    coef_shape = shape((planes, half_channels // SUB, 2 * cells * SUB, LANES), F32)
    inv_shape = shape((planes, half_channels // SUB, cells * SUB, LANES), F32)
    lhs_scr = pltpu.VMEM((planes, cells, channels, LANES), F32)
    span_scr = pltpu.VMEM((pieces_of, STEP, channels, span), F32)
    sem_scr = pltpu.SemaphoreType.DMA((pieces_of * STEP // PART + 1,))
    down = shape((2, total_modes * SUB, 2 * cells * SUB), BF16)
    back = shape((2, 2 * cells * SUB, total_modes * SUB), BF16)
    here = pl.BlockSpec(memory_space=pltpu.VMEM)
    apart = pl.BlockSpec(memory_space=pl.ANY)
    own_shape = shape((owned, planes, half_channels, LANES), F32)
    half_shape = shape((half_modes, planes, half_channels, LANES), F32)
    grid_shape = shape(x.shape, F32)

    send, coef, down, back = pl.pallas_call(
        functools.partial(spanwise_kernel, (owned, total_modes, cells)),
        in_specs=[apart, apart],
        out_specs=[here] * 4,
        out_shape=[half_shape, coef_shape, down, back],
        scratch_shapes=[pltpu.VMEM(ana_fwd.shape, BF16), span_scr, sem_scr],
        compiler_params=params(),
        name="spanwise",
    )(pltpu.with_memory_space_constraint(x, pltpu.HBM), pltpu.with_memory_space_constraint(ana_fwd, pltpu.HBM))

    def keep_part(coef):
        return lambda: pl.pallas_call(
            keep_kernel,
            in_specs=[here] * 2,
            out_specs=here,
            out_shape=half_shape,
            compiler_params=params(),
            name="keep_part",
        )(coef, down)

    def front_part(front):
        return pl.pallas_call(
            front_kernel,
            in_specs=[here] * 2,
            out_specs=here,
            out_shape=inv_shape,
            compiler_params=params(),
            name="front_part",
        )(front, back)

    def local_forward():
        return pl.pallas_call(
            functools.partial(pointwise_kernel, True),
            in_specs=[here] * 3,
            out_specs=here,
            out_shape=grid_shape,
            compiler_params=params(),
            name="local_forward",
        )(x, local_weight, offset_bias[None])

    pieces, local = scatter_sum(send, keep_part(coef), local_forward)
    modes, mixed = pl.pallas_call(
        mix_kernel,
        in_specs=[here] * (len(pieces) + 1),
        out_specs=[here] * 2,
        out_shape=[own_shape] * 2,
        compiler_params=params(),
        name="mix",
    )(*pieces, mode_weight)
    behind, inv, _ = gather_all(mixed, front_part)
    act, dpre, send, coef = pl.pallas_call(
        middle_kernel,
        in_specs=[here] * 8,
        out_specs=[here] * 4,
        out_shape=[grid_shape, grid_shape, half_shape, coef_shape],
        scratch_shapes=[lhs_scr],
        compiler_params=params(),
        name="middle",
    )(local, up, behind, inv, syn_inv, ana_inv, down, back)

    def local_backward():
        return pl.pallas_call(
            lambda values, weight, out: pointwise_kernel(False, values, weight, None, out),
            in_specs=[here] * 2,
            out_specs=here,
            out_shape=grid_shape,
            compiler_params=params(),
            name="local_backward",
        )(dpre, local_weight)

    pieces, local = scatter_sum(send, keep_part(coef), local_backward)
    dmixed, dmodes = pl.pallas_call(
        adjoint_kernel,
        in_specs=[here] * (len(pieces) + 1),
        out_specs=[here] * 2,
        out_shape=[own_shape] * 2,
        compiler_params=params(),
        name="adjoint",
    )(*pieces, mode_weight)

    def weight_grad():
        return pl.pallas_call(
            weight_grad_kernel,
            in_specs=[here] * 2,
            out_specs=here,
            out_shape=shape(mode_weight.shape, F32),
            compiler_params=params(),
            name="weight_grad",
        )(modes, dmixed)

    behind, inv, grad_modes = gather_all(dmodes, front_part, weight_grad)
    grad_snapshot = pl.pallas_call(
        input_grad_kernel,
        in_specs=[here] * 5,
        out_specs=apart,
        out_shape=grid_shape,
        scratch_shapes=[span_scr, lhs_scr, sem_scr],
        compiler_params=params(),
        name="input_grad",
    )(local, behind, inv, syn_fwd, back)
    return jnp.swapaxes(act, 2, 3), jnp.swapaxes(grad_snapshot, 2, 3), grad_modes


def solution(mesh):
    wide = P("stream", "group", None, None)
    return jax.shard_map(
        per_device,
        mesh=mesh,
        in_specs=(wide, P("stream", None, None, None), P(), P(), wide),
        out_specs=(wide, wide, wide),
        check_vma=False,
    )
```
